32 devices in a mesh: dp: 8 (over z, x), ctx: 4 (over y, core).
Axes of the slice: x: 2, y: 2, z: 4, core: 2. Of those that a mesh axis runs over, the one named last changes fastest.
Arguments:
- block_input: bfloat16 [8, 512, 1088], P('dp', 'ctx'), may hold values from -6 to 6
- norm_one_gain: bfloat16 [1088], P('dp'), may hold values from 0.099609375 to 1.8984375
- norm_one_bias: bfloat16 [1088], P('dp'), may hold values from -1.796875 to 1.796875
- w_qkv: bfloat16 [1088, 3264], P('ctx', 'dp'), may hold values from -3 to 3
- bias_qv: bfloat16 [2176], P('dp'), may hold values from -1.1953125 to 1.1953125
- w_out: bfloat16 [1088, 1088], P('ctx', 'dp'), may hold values from -1.5 to 1.5
- bias_out: bfloat16 [1088], P('dp'), may hold values from -1.796875 to 1.796875
- norm_two_gain: bfloat16 [1088], P('dp'), may hold values from 0.099609375 to 1.8984375
- norm_two_bias: bfloat16 [1088], P('dp'), may hold values from -1.796875 to 1.796875
- w_up: bfloat16 [1088, 4352], P('ctx', 'dp'), may hold values from -0.1875 to 0.1875
- bias_up: bfloat16 [4352], P('dp'), may hold values from -1.796875 to 1.796875
- w_down: bfloat16 [4352, 1088], P('ctx', 'dp'), may hold values from -0.09375 to 0.09375
- bias_down: bfloat16 [1088], P('dp'), may hold values from -1.796875 to 1.796875
- cotangent: bfloat16 [8, 512, 1088], P('dp', 'ctx'), may hold values from -6 to 6
Outputs:
- block_output: bfloat16 [8, 512, 1088], P('dp', 'ctx')
- grad_input: float32 [8, 512, 1088], P('dp', 'ctx')
- grad_norm_one_gain: float32 [1088], P('dp')
- grad_norm_one_bias: float32 [1088], P('dp')
- grad_w_qkv: float32 [1088, 3264], P('ctx', 'dp')
- grad_bias_qv: float32 [2176], P('dp')
- grad_w_out: float32 [1088, 1088], P('ctx', 'dp')
- grad_bias_out: float32 [1088], P('dp')
- grad_norm_two_gain: float32 [1088], P('dp')
- grad_norm_two_bias: float32 [1088], P('dp')
- grad_w_up: float32 [1088, 4352], P('ctx', 'dp')
- grad_bias_up: float32 [4352], P('dp')
- grad_w_down: float32 [4352, 1088], P('ctx', 'dp')
- grad_bias_down: float32 [1088], P('dp')
The draws below stay inside these ranges and needn't reach their ends.
All inputs are finite; a program needn't handle non-finite values.
Results may differ from the reference program's by a relative error of at most 0.01.
Values may be sent and summed in bfloat16 or wider, within the bound.
A program may use at most 192 MiB of HBM per device.

```python
import jax
import jax.numpy as jnp
from jax import lax

D = 1088
HEADS = 17
HEAD_DIM = 64
FF = 4352
LENGTH = 512
SEQS = 8
TOKENS = 4096


def draw_w_qkv(key, part):
    standard = jax.random.truncated_normal(key, -4.0, 4.0, (D, 3 * D), jnp.float32) * float(D) ** (-0.5)
    return standard.astype(jnp.bfloat16)


def strengthened(values, rng, source, target, shards_of, factor):
    owner, partner = [(jnp.arange(values.shape[axis_at]) // (values.shape[axis_at] // shards_of)).reshape([-1 if axis == axis_at else 1 for axis in range(values.ndim)]) for axis_at in (source, target)]
    chosen = jax.random.permutation(rng, shards_of)[partner]
    strong = (owner == chosen) | (owner == (partner + shards_of // 2) % shards_of)
    return jnp.where(strong, factor * values, values)


def block_levels(key, extent, cuts, least, largest):
    def one(axis_at, parts):
        heights = jax.random.uniform(jax.random.fold_in(jax.random.fold_in(key, 6), axis_at), (parts,), jnp.float32, least / len(cuts), largest / len(cuts))
        return jnp.repeat(jnp.exp(heights), extent[axis_at] // parts).reshape((-1,) + (1,) * (len(extent) - axis_at - 1))

    loudness = one(*cuts[0])
    for cut in cuts[1:]:
        loudness = loudness * one(*cut)
    return loudness


def centred(stream_key, dims, deviation, bound, cuts=(), kind=jnp.bfloat16):
    level = block_levels(stream_key, dims, cuts, -0.22, 0.18) if cuts else 1.0
    values = jax.random.normal(stream_key, dims, jnp.float32) * deviation * level
    return jnp.minimum(jnp.maximum(values, -bound), bound).astype(kind)


def bell_draw_with(rng, shape, scale, most, split, heavy, held_as=jnp.bfloat16):
    values = scale * jax.random.normal(rng, shape, jnp.float32)
    if split:
        values = values * block_levels(rng, shape, split, -0.22, 0.18)
    return jnp.clip(strengthened(values, jax.random.fold_in(rng, 3), *heavy), -most, most).astype(held_as)


def setup_inputs(seed: int = 0) -> dict:
    arg_keys = jax.random.split(jax.random.key(seed), 15)
    return {
        "block_input": centred(arg_keys[0], (SEQS, LENGTH, D), 1.0, 6.0, ((0, 8), (1, 4))),
        "norm_one_gain": jnp.clip(1.0 + 0.18 * jax.random.normal(arg_keys[1], (D,), jnp.float32), 0.099609375, 1.8984375).astype(jnp.bfloat16),
        "norm_one_bias": centred(arg_keys[2], (D,), 0.3, 1.796875, ((0, 8),)),
        "w_qkv": draw_w_qkv(jax.random.fold_in(arg_keys[14], 71), 0),
        "bias_qv": centred(arg_keys[4], (2 * D,), 0.2, 1.1953125, ((0, 8),)),
        "w_out": centred(arg_keys[5], (D, D), (D // 64) ** -0.5, 1.5, ((0, 4), (1, 8))),
        "bias_out": centred(arg_keys[6], (D,), 0.3, 1.796875, ((0, 8),)),
        "norm_two_gain": jnp.clip(1.0 + 0.18 * jax.random.normal(arg_keys[7], (D,), jnp.float32), 0.099609375, 1.8984375).astype(jnp.bfloat16),
        "norm_two_bias": centred(arg_keys[8], (D,), 0.3, 1.796875, ((0, 8),)),
        "w_up": centred(arg_keys[9], (D, FF), D ** -0.5, 0.1875, ((0, 4), (1, 8))),
        "bias_up": centred(arg_keys[10], (FF,), 0.3, 1.796875, ((0, 8),)),
        "w_down": centred(arg_keys[11], (FF, D), FF ** -0.5, 0.09375, ((0, 4), (1, 8))),
        "bias_down": centred(arg_keys[12], (D,), 0.3, 1.796875, ((0, 8),)),
        "cotangent": bell_draw_with(arg_keys[13], (SEQS, LENGTH, D), 1.0, 6.0, ((0, 8), (1, 4)), (0, 2, 8, 2.0)),
    }


EPS = 1e-05
MASKED = -1e+30
INV_ROOT_TWO = 0.7071067811865476
INV_ROOT_TWO_PI = 0.3989422804014327

def norm_forward(rows_in, gain, shift):
    center = lax.optimization_barrier(jnp.mean(rows_in, axis=-1, keepdims=True))
    offset = rows_in - center
    spread = lax.optimization_barrier(jnp.mean(offset * offset, axis=-1, keepdims=True))
    inverse = lax.rsqrt(spread + EPS)
    scaled = offset * inverse
    normed = (scaled * gain.astype(jnp.float32) + shift.astype(jnp.float32)).astype(jnp.bfloat16)
    return (scaled, inverse, normed)

def norm_backward(upstream, scaled, inverse, gain):
    weighted = upstream * gain.astype(jnp.float32)
    first = lax.optimization_barrier(jnp.mean(weighted, axis=-1, keepdims=True))
    second = lax.optimization_barrier(jnp.mean(weighted * scaled, axis=-1, keepdims=True))
    return inverse * (weighted - first - scaled * second)

def gelu_value(pre):
    return 0.5 * pre * (1.0 + lax.erf(pre * INV_ROOT_TWO))

def gelu_slope(pre):
    return 0.5 * (1.0 + lax.erf(pre * INV_ROOT_TWO)) + pre * jnp.exp(-0.5 * pre * pre) * INV_ROOT_TWO_PI

def split_heads(block):
    return block.astype(jnp.float32).reshape(block.shape[0], HEADS, HEAD_DIM)

def reference(block_input, norm_one_gain, norm_one_bias, w_qkv, bias_qv, w_out, bias_out, norm_two_gain, norm_two_bias, w_up, bias_up, w_down, bias_down, cotangent):
    factor = float(HEAD_DIM) ** (-0.5)
    bias_float = bias_qv.astype(jnp.float32)
    qkv_bias = jnp.concatenate([bias_float[:D], jnp.zeros((D,), jnp.float32), bias_float[D:]])
    positions = jnp.arange(LENGTH, dtype=jnp.int32)
    allowed = positions[None, :] <= positions[:, None]

    def one_sequence(totals, pair):
        seq_in, seq_cot = pair
        inputs = seq_in.astype(jnp.float32)
        scaled_one, inverse_one, normed_one = norm_forward(inputs, norm_one_gain, norm_one_bias)
        projected = (jnp.dot(normed_one, w_qkv, preferred_element_type=jnp.float32) + qkv_bias).astype(jnp.bfloat16)
        query_heads = split_heads(projected[:, :D])
        key_heads = split_heads(projected[:, D:2 * D])
        value_heads = split_heads(projected[:, 2 * D:])
        scores = jnp.einsum('qhd,khd->hqk', query_heads, key_heads) * factor
        scores = jnp.where(allowed[None], scores, MASKED)
        peak = lax.optimization_barrier(jnp.max(scores, axis=-1, keepdims=True))
        log_total = peak + jnp.log(lax.optimization_barrier(jnp.sum(jnp.exp(scores - peak), axis=-1, keepdims=True)))
        probs = jnp.exp(scores - log_total)
        soft_weights = probs.astype(jnp.bfloat16)
        mixed = jnp.einsum('hqk,khd->qhd', soft_weights.astype(jnp.float32), value_heads).reshape(LENGTH, D).astype(jnp.bfloat16)
        residual = inputs + (jnp.dot(mixed, w_out, preferred_element_type=jnp.float32) + bias_out.astype(jnp.float32))
        scaled_two, inverse_two, normed_two = norm_forward(residual, norm_two_gain, norm_two_bias)
        hidden_pre = jnp.dot(normed_two, w_up, preferred_element_type=jnp.float32) + bias_up.astype(jnp.float32)
        hidden = gelu_value(hidden_pre).astype(jnp.bfloat16)
        result = residual + (jnp.dot(hidden, w_down, preferred_element_type=jnp.float32) + bias_down.astype(jnp.float32))
        output = result.astype(jnp.bfloat16)
        up_float = seq_cot.astype(jnp.float32)
        grad_down = jnp.dot(hidden.T, seq_cot, preferred_element_type=jnp.float32)
        grad_bias_down = lax.optimization_barrier(jnp.sum(up_float, axis=0))
        grad_hidden = jnp.dot(seq_cot, w_down.T, preferred_element_type=jnp.float32) * gelu_slope(hidden_pre)
        grad_hidden_low = grad_hidden.astype(jnp.bfloat16)
        grad_up = jnp.dot(normed_two.T, grad_hidden_low, preferred_element_type=jnp.float32)
        grad_bias_up = lax.optimization_barrier(jnp.sum(grad_hidden, axis=0))
        grad_normed_two = jnp.dot(grad_hidden_low, w_up.T, preferred_element_type=jnp.float32)
        grad_gain_two = lax.optimization_barrier(jnp.sum(grad_normed_two * scaled_two, axis=0))
        grad_shift_two = lax.optimization_barrier(jnp.sum(grad_normed_two, axis=0))
        grad_residual = up_float + norm_backward(grad_normed_two, scaled_two, inverse_two, norm_two_gain)
        grad_residual_low = grad_residual.astype(jnp.bfloat16)
        grad_out = jnp.dot(mixed.T, grad_residual_low, preferred_element_type=jnp.float32)
        grad_bias_out = lax.optimization_barrier(jnp.sum(grad_residual, axis=0))
        grad_mixed = jnp.dot(grad_residual_low, w_out.T, preferred_element_type=jnp.float32).astype(jnp.bfloat16)
        mixed_heads = split_heads(grad_mixed)
        grad_probs = jnp.einsum('qhd,khd->hqk', mixed_heads, value_heads)
        delta = jnp.einsum('qhd,qhd->hq', mixed_heads, split_heads(mixed))[..., None]
        grad_scores = (probs * (grad_probs - delta) * factor).astype(jnp.bfloat16).astype(jnp.float32)
        grad_queries = jnp.einsum('hqk,khd->qhd', grad_scores, key_heads).reshape(LENGTH, D)
        grad_keys = jnp.einsum('hqk,qhd->khd', grad_scores, query_heads).reshape(LENGTH, D)
        grad_values = jnp.einsum('hqk,qhd->khd', soft_weights.astype(jnp.float32), mixed_heads).reshape(LENGTH, D)
        grad_bias_qv = jnp.concatenate([lax.optimization_barrier(jnp.sum(grad_queries, axis=0)), lax.optimization_barrier(jnp.sum(grad_values, axis=0))])
        grad_projected = jnp.concatenate([grad_queries, grad_keys, grad_values], axis=1).astype(jnp.bfloat16)
        grad_qkv = jnp.dot(normed_one.T, grad_projected, preferred_element_type=jnp.float32)
        grad_normed_one = jnp.dot(grad_projected, w_qkv.T, preferred_element_type=jnp.float32)
        grad_gain_one = lax.optimization_barrier(jnp.sum(grad_normed_one * scaled_one, axis=0))
        grad_shift_one = lax.optimization_barrier(jnp.sum(grad_normed_one, axis=0))
        grad_in = grad_residual + norm_backward(grad_normed_one, scaled_one, inverse_one, norm_one_gain)
        terms = (grad_gain_one, grad_shift_one, grad_qkv, grad_bias_qv, grad_out, grad_bias_out, grad_gain_two, grad_shift_two, grad_up, grad_bias_up, grad_down, grad_bias_down)
        new_totals = tuple((total + term for total, term in zip(totals, terms)))
        return (new_totals, (output, grad_in))
    start = (jnp.zeros((D,), jnp.float32), jnp.zeros((D,), jnp.float32), jnp.zeros((D, 3 * D), jnp.float32), jnp.zeros((2 * D,), jnp.float32), jnp.zeros((D, D), jnp.float32), jnp.zeros((D,), jnp.float32), jnp.zeros((D,), jnp.float32), jnp.zeros((D,), jnp.float32), jnp.zeros((D, FF), jnp.float32), jnp.zeros((FF,), jnp.float32), jnp.zeros((FF, D), jnp.float32), jnp.zeros((D,), jnp.float32))
    totals, stacked = lax.scan(one_sequence, start, (block_input, cotangent))
    outputs, grad_inputs = stacked
    scale = float(TOKENS) ** (-0.5)
    return (outputs, grad_inputs, totals[0] * scale, totals[1] * scale, totals[2] * scale, totals[3] * scale, totals[4] * scale, totals[5] * scale, totals[6] * scale, totals[7] * scale, totals[8] * scale, totals[9] * scale, totals[10] * scale, totals[11] * scale)
```

```python
import functools

import jax
import jax.numpy as jnp
import numpy as np
from jax import lax
from jax.experimental import pallas as pl
from jax.experimental.pallas import tpu as pltpu
from jax.sharding import PartitionSpec as P

HEADS = 17
HEAD_DIM = 64
HEAD_GROUP = (0, 2, 1, 3, 2, 0, 1, 3, 0, 1, 2, 0, 3, 3, 2, 0, 1)

EPS = 1e-05
MASKED = -1e30
INV_ROOT_TWO = 0.7071067811865476
INV_ROOT_TWO_PI = 0.3989422804014327

F32 = jnp.float32
LOW = jnp.bfloat16
VMEM_LIMIT = 60 * 1024 * 1024


def norm_stats(rows_in):
    center = jnp.mean(rows_in, axis=-1, keepdims=True)
    offset = rows_in - center
    spread = jnp.mean(offset * offset, axis=-1, keepdims=True)
    inverse = lax.rsqrt(spread + EPS)
    return offset * inverse, inverse


def norm_backward(upstream, scaled, inverse, gain):
    weighted = upstream * gain
    first = jnp.mean(weighted, axis=-1, keepdims=True)
    second = jnp.mean(weighted * scaled, axis=-1, keepdims=True)
    return inverse * (weighted - first - scaled * second)


def gelu_value(pre):
    return 0.5 * pre * (1.0 + lax.erf(pre * INV_ROOT_TWO))


def gelu_slope(pre):
    return (
        0.5 * (1.0 + lax.erf(pre * INV_ROOT_TWO))
        + pre * jnp.exp(-0.5 * pre * pre) * INV_ROOT_TWO_PI
    )


def inner_rows(left, right):
    return lax.dot_general(left, right, (((0,), (0,)), ((), ())), preferred_element_type=F32)


def outer_cols(left, right):
    return lax.dot_general(left, right, (((1,), (1,)), ((), ())), preferred_element_type=F32)


def plain(left, right):
    return jnp.dot(left, right, preferred_element_type=F32)


def rounded_up(value, step):
    return -(-value // step) * step


def slot_tables(width, dp, ctx):
    group = np.array(HEAD_GROUP)
    heads_of = [np.flatnonzero(group == g) for g in range(ctx)]
    most = max(len(h) for h in heads_of)
    head_rows = np.full((ctx, most), -1, np.int32)
    for g in range(ctx):
        head_rows[g, : len(heads_of[g])] = heads_of[g]

    wide = 3 * width // dp
    column = np.arange(3 * width)
    column_group = group[(column % width) // HEAD_DIM]
    column_dp = column // wide
    lists = [
        [column[(column_dp == d) & (column_group == g)] for g in range(ctx)] for d in range(dp)
    ]
    slot = rounded_up(max(len(v) for row in lists for v in row), 128)
    column_pick = np.full((dp, ctx * slot), -1, np.int32)
    place = np.full((3 * width,), -1, np.int32)
    for d in range(dp):
        for g in range(ctx):
            v = lists[d][g]
            column_pick[d, g * slot : g * slot + len(v)] = v - d * wide
            place[v] = d * slot + np.arange(len(v))
    head_pick = np.full((ctx, 3, most, HEAD_DIM), -1, np.int32)
    for g in range(ctx):
        for i, h in enumerate(heads_of[g]):
            for t in range(3):
                at = t * width + h * HEAD_DIM
                head_pick[g, t, i] = place[at : at + HEAD_DIM]
    head_pick = head_pick.reshape(ctx, -1)

    high = width // ctx
    row = np.arange(width)
    row_group = group[row // HEAD_DIM]
    row_lists = [[row[(row // high == r) & (row_group == g)] for g in range(ctx)] for r in range(ctx)]
    row_pack = rounded_up(max(len(v) for one in row_lists for v in one), 32)
    row_slot = rounded_up(row_pack, 128)
    row_pick = np.full((ctx, ctx * row_slot), -1, np.int32)
    row_place = np.full((width,), -1, np.int32)
    for r in range(ctx):
        for g in range(ctx):
            v = row_lists[r][g]
            row_pick[r, g * row_slot : g * row_slot + len(v)] = v - r * high
            row_place[v] = r * row_pack + np.arange(len(v))
    mixed_pick = np.full((ctx, most, HEAD_DIM), -1, np.int32)
    for g in range(ctx):
        for i, h in enumerate(heads_of[g]):
            mixed_pick[g, i] = row_place[h * HEAD_DIM : (h + 1) * HEAD_DIM]
    return dict(
        most=most,
        slot=slot,
        row_slot=row_slot,
        row_pack=row_pack,
        head_rows=head_rows,
        column_pick=column_pick,
        head_pick=head_pick,
        row_pick=row_pick,
        mixed_pick=mixed_pick.reshape(ctx, -1),
    )


def picker(table, which, size, dtype=LOW):
    chosen = lax.dynamic_index_in_dim(jnp.asarray(table), which, 0, keepdims=False)
    return (jnp.arange(size, dtype=jnp.int32)[:, None] == chosen[None, :]).astype(dtype)


def row_picker(table, which, size, dtype=LOW):
    chosen = lax.dynamic_index_in_dim(jnp.asarray(table), which, 0, keepdims=False)
    return (chosen[:, None] == jnp.arange(size, dtype=jnp.int32)[None, :]).astype(dtype)


class Net:
    def __init__(self, send_sem, recv_sem):
        self.send_sem, self.recv_sem = send_sem, recv_sem
        self.used = 0
        self.dp = lax.axis_size("dp")
        self.ctx = lax.axis_size("ctx")
        self.inner = 2
        self.outer = self.dp // self.inner
        self.d = lax.axis_index("dp")
        self.c = lax.axis_index("ctx")
        self.z = self.d // self.inner
        self.x = lax.rem(self.d, self.inner)
        self.beside = self.z * self.inner + (1 - self.x)
        self.partner = self.c + 1 - 2 * lax.rem(self.c, 2)
        self.across = lax.rem(self.c + 2, 4)
        self.corner = lax.rem(self.partner + 2, 4)

    def at(self, z):
        return z * self.inner + self.x

    def greet(self):
        barrier = pltpu.get_barrier_semaphore()
        self.signal(barrier, {"dp": self.beside})
        for step in range(1, self.ctx):
            self.signal(barrier, {"ctx": lax.rem(self.c + step, self.ctx)})

        @pl.when(self.z > 0)
        def _():
            self.signal(barrier, {"dp": self.at(self.z - 1)})

        @pl.when(self.z < self.outer - 1)
        def _():
            self.signal(barrier, {"dp": self.at(self.z + 1)})

        ends = jnp.where(self.z > 0, 1, 0) + jnp.where(self.z < self.outer - 1, 1, 0)
        pl.semaphore_wait(barrier, self.ctx + ends)

    @staticmethod
    def signal(barrier, device):
        pl.semaphore_signal(
            barrier, inc=1, device_id=device, device_id_type=pl.DeviceIdType.MESH
        )

    def room(self, count):
        at = self.used
        self.used += count
        return at

    def copy(self, at, source, dest, **device):
        return pltpu.make_async_remote_copy(
            src_ref=source,
            dst_ref=dest,
            send_sem=self.send_sem.at[at],
            recv_sem=self.recv_sem.at[at],
            device_id=device,
            device_id_type=pl.DeviceIdType.MESH,
        )

    def send(self, source, dest, **device):
        copy = self.copy(self.room(1), source, dest, **device)
        copy.start()
        return copy


class Gather:
    def __init__(self, net, place, hop=True):
        self.net, self.place, self.hop = net, place, hop
        links = net.outer - 1
        self.right, self.left = net.room(links), net.room(links)
        self.hop_right, self.hop_left = net.room(links), net.room(links)
        if hop:
            mine = place(net.z)
            self.own = net.send(mine, mine, dp=net.beside)
        self.pass_on(0, net.z, net.z < net.outer - 1, net.z > 0)

    def moving(self, base, k, z, toward):
        view = self.place(z)
        return self.net.copy(base + k, view, view, dp=self.net.at(self.net.z + toward))

    def beside(self, base, k, z):
        view = self.place(z)
        return self.net.copy(base + k, view, view, dp=self.net.beside)

    def pass_on(self, k, z, right, left):
        if k >= self.net.outer - 1:
            return
        if right is not None:

            @pl.when(right)
            def _():
                self.moving(self.right, k, z, 1).start()

        if left is not None:

            @pl.when(left)
            def _():
                self.moving(self.left, k, z, -1).start()

    def step(self, k):
        net = self.net
        from_left, from_right = net.z - 1 - k, net.z + 1 + k

        @pl.when(from_left >= 0)
        def _():
            self.moving(self.right, k, from_left, -1).wait_recv()
            self.pass_on(k + 1, from_left, net.z < net.outer - 1, None)
            if self.hop:
                self.beside(self.hop_right, k, from_left).start()

        @pl.when(from_right < net.outer)
        def _():
            self.moving(self.left, k, from_right, 1).wait_recv()
            self.pass_on(k + 1, from_right, None, net.z > 0)
            if self.hop:
                self.beside(self.hop_left, k, from_right).start()

    def finish(self):
        net = self.net
        if self.hop:
            self.own.wait()
        for k in range(net.outer - 1):
            here_left, here_right = net.z - k, net.z + k

            @pl.when((here_left >= 0) & (net.z < net.outer - 1))
            def _():
                self.moving(self.right, k, here_left, 1).wait_send()

            @pl.when((here_right < net.outer) & (net.z > 0))
            def _():
                self.moving(self.left, k, here_right, -1).wait_send()

            if self.hop:

                @pl.when(net.z - 1 - k >= 0)
                def _():
                    self.beside(self.hop_right, k, net.z - 1 - k).wait()

                @pl.when(net.z + 1 + k < net.outer)
                def _():
                    self.beside(self.hop_left, k, net.z + 1 + k).wait()


class PairGather:
    def __init__(self, net, mine, pair):
        self.net, self.pair = net, pair
        self.own = net.send(mine, mine, dp=net.beside)

    def begin(self):
        self.own.wait()
        self.chain = Gather(self.net, self.pair, hop=False)

    def step(self, k):
        self.chain.step(k)

    def finish(self):
        self.chain.finish()


class Scatter:
    def __init__(self, net, source, near, passed, acc):
        self.net, self.source, self.near, self.passed, self.acc = net, source, near, passed, acc
        self.hop = net.room(net.outer)
        self.right, self.left = net.room(net.outer), net.room(net.outer)
        for k in range(net.outer - 1):
            self.each(k, lambda flow, z: self.over(z).start())
        self.over(net.z).start()

    def each(self, k, act):
        net = self.net
        back = net.outer - 1 - net.z

        @pl.when(k >= net.z)
        def _():
            act(1, net.outer - 1 - (k - net.z))

        @pl.when(k >= back)
        def _():
            act(-1, k - back)

    def over(self, z):
        return self.net.copy(
            self.hop + z, self.source(z, 1 - self.net.x), self.near.at[z], dp=self.net.beside
        )

    def term(self, z):
        return self.source(z, self.net.x)[...].astype(F32) + self.near[z].astype(F32)

    def slot(self, flow, z, here):
        if flow > 0:
            return z
        return jnp.where(z < here, z, self.net.outer)

    def moving(self, flow, z):
        net = self.net
        base = self.right if flow > 0 else self.left
        there = net.z + flow
        return net.copy(
            base + z, self.near.at[z], self.passed.at[self.slot(flow, z, there)], dp=net.at(there)
        )

    def arrived(self, flow, z):
        net = self.net
        base = self.right if flow > 0 else self.left
        slot = self.slot(flow, z, net.z)
        net.copy(
            base + z, self.near.at[z], self.passed.at[slot], dp=net.at(net.z - flow)
        ).wait_recv()
        return slot

    def push(self, flow, z):
        net = self.net
        first = net.z == (0 if flow > 0 else net.outer - 1)
        self.over(z).wait_recv()

        @pl.when(first)
        def _():
            self.near[z] = self.term(z).astype(self.near.dtype)

        @pl.when(jnp.logical_not(first))
        def _():
            slot = self.arrived(flow, z)
            self.near[z] = (self.term(z) + self.passed[slot].astype(F32)).astype(self.near.dtype)

        self.moving(flow, z).start()

    def step(self, k):
        self.each(k, self.push)

    def total(self):
        net = self.net
        self.over(net.z).wait_recv()
        self.acc[...] = self.term(net.z)

        @pl.when(net.z > 0)
        def _():
            self.acc[...] += self.passed[self.arrived(1, net.z)].astype(F32)

        @pl.when(net.z < net.outer - 1)
        def _():
            self.acc[...] += self.passed[self.arrived(-1, net.z)].astype(F32)

    def finish(self):
        net = self.net
        self.over(net.z).wait_send()
        for z in range(net.outer):

            @pl.when(net.z != z)
            def _():
                self.over(z).wait_send()

            @pl.when(z > net.z)
            def _():
                self.moving(1, z).wait_send()

            @pl.when(z < net.z)
            def _():
                self.moving(-1, z).wait_send()


class Share:
    def __init__(self, net, whole, chunks=4):
        self.net, self.whole = net, whole
        size = whole.shape[1] // chunks
        self.spans = [pl.ds(part * size, size) for part in range(chunks)]
        self.far = [self.send(net.c, s, net.across) for s in self.spans]
        self.near = [self.send(net.c, s, net.partner) for s in self.spans]
        self.handed = []

    def send(self, slot, span, target):
        view = self.whole.at[slot, span]
        return self.net.send(view, view, ctx=target)

    def forward(self):
        for part, s in enumerate(self.spans):
            self.far[part].wait_recv()
            self.handed.append(self.send(self.net.across, s, self.net.partner))

    def finish(self):
        for part in range(len(self.spans)):
            self.far[part].wait_send()
            self.near[part].wait()
            self.handed[part].wait()


class Fold:
    def __init__(self, net, parts, near, held, far, make=None, chunks=4):
        self.net, self.parts, self.near, self.held, self.far_in = net, parts, near, held, far
        size = parts.shape[1] // chunks
        self.spans = [pl.ds(part * size, size) for part in range(chunks)]
        make = make or (lambda owner: None)
        make(net.corner)
        self.first = [
            net.send(parts.at[net.corner, s], near.at[0, s], ctx=net.partner) for s in self.spans
        ]
        make(net.across)
        self.far = []
        for part, s in enumerate(self.spans):
            self.first[part].wait_recv()
            self.held[s] = (
                self.parts[net.across, s].astype(F32) + self.near[0, s].astype(F32)
            ).astype(LOW)
            self.far.append(net.send(self.held.at[s], self.far_in.at[s], ctx=net.across))
        make(net.partner)
        self.own = [
            net.send(parts.at[net.partner, s], near.at[1, s], ctx=net.partner) for s in self.spans
        ]
        make(net.c)

    def total(self, out):
        net = self.net
        for part, s in enumerate(self.spans):
            self.own[part].wait_recv()
            out[s] = self.parts[net.c, s].astype(F32) + self.near[1, s].astype(F32)
        for part, s in enumerate(self.spans):
            self.far[part].wait_recv()
            out[s] = out[s] + self.far_in[s].astype(F32)

    def finish(self):
        for part in range(len(self.spans)):
            self.first[part].wait_send()
            self.own[part].wait_send()
            self.far[part].wait_send()


class Trade:
    def __init__(self, net, block, place):
        self.copies = []
        for step in (2, 1, 3):
            target = lax.rem(net.c + step, net.ctx)
            self.copies.append(net.send(block.at[target], place(net.c), ctx=target))

    def received(self):
        for copy in self.copies:
            copy.wait_recv()

    def finish(self):
        for copy in self.copies:
            copy.wait_send()


def fold_scratch(rows, wide):
    return [
        pltpu.VMEM((2, rows, wide), LOW),
        pltpu.VMEM((rows, wide), LOW),
        pltpu.VMEM((rows, wide), LOW),
    ]


def net_call(kernel, ident, name, ins, outs, scratch=(), copies=64, cost=None):
    return pl.pallas_call(
        kernel,
        out_shape=[jax.ShapeDtypeStruct(s, t) for s, t in outs],
        in_specs=[pl.BlockSpec(memory_space=pltpu.VMEM)] * len(ins),
        out_specs=[pl.BlockSpec(memory_space=pltpu.VMEM)] * len(outs),
        scratch_shapes=[
            *scratch,
            pltpu.SemaphoreType.DMA((copies,)),
            pltpu.SemaphoreType.DMA((copies,)),
        ],
        compiler_params=pltpu.CompilerParams(
            collective_id=ident, has_side_effects=True, vmem_limit_bytes=VMEM_LIMIT
        ),
        name=name,
    )(*ins)


def first_kernel(
    fused,
    x_ref, cot_ref, wq_ref, wo_ref, up_ref, down_ref, vec_ref,
    x_all, wq_all, up_mine, down_mine, vec_all, wo_all, *rest,
):
    cot_all = None if fused else rest[0]
    wo_got, send_sem, recv_sem = rest[-3:]
    net = Net(send_sem, recv_sem)
    d, c = net.d, net.c
    vec_all[d] = vec_ref[...]
    wq_all[d, c] = wq_ref[c]
    wo_got[c] = wo_ref[c]
    x_all[c] = x_ref[...]
    if not fused:
        cot_all[c] = cot_ref[...]
    net.greet()
    trade_q = Trade(net, wq_ref, lambda r: wq_all.at[d, r])
    vectors = PairGather(net, vec_all.at[d], lambda z: vec_all.at[pl.ds(z * 2, 2)])
    trade_o = Trade(net, wo_ref, lambda r: wo_got.at[r])
    share_x = Share(net, x_all)
    up_mine[c] = up_ref[c]
    down_mine[c] = down_ref[c]
    trade_q.received()
    gather_q = Gather(net, lambda z: wq_all.at[net.at(z)])
    trade_o.received()
    wo_mine = wo_all.at[d]
    room = wo_mine.shape[1] // net.ctx
    for r in range(net.ctx):
        wo_mine[:, r * room : (r + 1) * room] = wo_got[r, :, :room]
    gather_o = PairGather(net, wo_mine, lambda z: wo_all.at[pl.ds(z * 2, 2)])
    vectors.begin()
    share_x.forward()
    trade_up = Trade(net, up_ref, lambda r: up_mine.at[r])
    trade_down = Trade(net, down_ref, lambda r: down_mine.at[r])
    items = [trade_q, trade_o, vectors, share_x, gather_q, gather_o, trade_up, trade_down]
    if not fused:
        share_cot = Share(net, cot_all)
        share_cot.forward()
        items.append(share_cot)
    gather_q.step(0)
    vectors.step(0)
    gather_o.begin()
    for k in range(1, net.outer - 1):
        gather_q.step(k)
        gather_o.step(k - 1)
        vectors.step(k)
    gather_o.step(net.outer - 2)
    trade_up.received()
    trade_down.received()
    for item in items:
        item.finish()


def second_kernel(
    parts, x_ref, up_ref, down_ref, bias_ref, gain_ref, shift_ref,
    up_all, down_all, normed_all, residual_ref,
    near, held, far, send_sem, recv_sem,
):
    net = Net(send_sem, recv_sem)
    d, c = net.d, net.c
    up_all[d] = up_ref[...]
    down_all[d] = down_ref[...]
    net.greet()
    fold = Fold(net, parts, near, held, far)
    ff = down_all.shape[2]
    cut = pair_cut(ff)
    gather_up = Gather(net, lambda z: up_all.at[net.at(z)])
    pair_down = PairGather(
        net, down_all.at[d, :, pl.ds(0, cut)], lambda z: down_all.at[pl.ds(z * 2, 2), :, pl.ds(0, cut)]
    )
    fold.total(residual_ref)
    gather_up.step(0)
    pair_down.begin()
    gather_down = Gather(net, lambda z: down_all.at[net.at(z), :, pl.ds(cut, ff - cut)])
    residual = x_ref[...].astype(F32) + (residual_ref[...] + bias_ref[...])
    residual_ref[...] = residual
    scaled, _ = norm_stats(residual)
    normed_all[c] = (scaled * gain_ref[...] + shift_ref[...]).astype(LOW)
    share = Share(net, normed_all)
    for k in range(net.outer - 1):
        if k > 0:
            gather_up.step(k)
        if k == 0:
            share.forward()
        pair_down.step(k)
        gather_down.step(k)
    for item in (fold, share, gather_up, gather_down, pair_down):
        item.finish()


def third_kernel(
    parts, residual_ref, cot_ref, down_grad, up_grad, bias_ref, gain_ref,
    block_out, grad_residual, normed_grad, low_all, down_mine, up_mine,
    sums, near, held, far, near_down, passed_down, near_up, passed_up, acc_down, acc_up, send_sem, recv_sem,
):
    net = Net(send_sem, recv_sem)
    c = net.c
    net.greet()
    fold = Fold(net, parts, near, held, far)
    scatter_down = Scatter(net, lambda z, x: down_grad.at[z * 2 + x], near_down, passed_down, acc_down)
    scatter_down.step(0)
    fold.total(sums)
    rows = residual_ref.shape[0]
    residual = residual_ref[...]
    block_out[...] = (residual + (sums[pl.ds(0, rows)] + bias_ref[...])).astype(LOW)
    scaled, inverse = norm_stats(residual)
    upstream = sums[pl.ds(rows, rows)]
    normed_grad[...] = upstream
    total = cot_ref[...].astype(F32) + norm_backward(upstream, scaled, inverse, gain_ref[...])
    grad_residual[...] = total
    low_all[c] = total.astype(LOW)
    share = Share(net, low_all)
    for k in range(1, net.outer - 2):
        scatter_down.step(k)
    share.forward()
    scatter_up = Scatter(net, lambda z, x: up_grad.at[z * 2 + x], near_up, passed_up, acc_up)
    scatter_down.step(net.outer - 2)
    for k in range(net.outer - 1):
        scatter_up.step(k)
    scatter_down.total()
    down_mine[...] = acc_down[...].astype(LOW)
    scatter_up.total()
    up_mine[...] = acc_up[...].astype(LOW)
    for item in (fold, share, scatter_down, scatter_up):
        item.finish()


def last_kernel(
    parts, wq_grad, wo_grad, lines_ref, bias_lines, up_ref, down_ref, x_ref, residual_grad, gain_ref,
    grad_input, wq_back, wo_back, totals, up_back, down_back,
    sums, near, held, far, near_q, passed_q, near_o, passed_o, near_t, passed_t,
    acc_q, acc_o, acc_t, wq_mine, wo_mine, lines, table, table_all, send_sem, recv_sem,
):
    net = Net(send_sem, recv_sem)
    c = net.c
    net.greet()
    fold = Fold(net, parts, near, held, far)
    scatter_q = Scatter(net, lambda z, x: wq_grad.at[z * 2 + x], near_q, passed_q, acc_q)
    trade_up = Trade(net, up_ref, lambda g: up_back.at[g])
    trade_down = Trade(net, down_ref, lambda g: down_back.at[g])
    up_back[c] = up_ref[c]
    down_back[c] = down_ref[c]
    scatter_q.step(0)
    scaled, inverse = norm_stats(x_ref[...].astype(F32))
    fold.total(sums)
    upstream = sums[...]
    grad_input[...] = residual_grad[...] + norm_backward(upstream, scaled, inverse, gain_ref[...])
    lines[...] = lines_ref[...]
    lines[0:1] = jnp.sum(upstream * scaled, axis=0, keepdims=True)
    lines[1:2] = jnp.sum(upstream, axis=0, keepdims=True)
    lines[2 : 2 + bias_lines.shape[0]] = bias_lines[...]
    part = table.shape[2]
    for p in range(net.dp):
        table[p] = lines[:, p * part : (p + 1) * part]
    for k in range(1, net.outer - 2):
        scatter_q.step(k)
    scatter_o = Scatter(net, lambda z, x: wo_grad.at[z * 2 + x], near_o, passed_o, acc_o)
    scatter_t = Scatter(net, lambda z, x: table.at[z * 2 + x], near_t, passed_t, acc_t)
    scatter_q.step(net.outer - 2)
    for k in range(net.outer - 1):
        scatter_o.step(k)
        scatter_t.step(k)
    scatter_q.total()
    wq_mine[...] = acc_q[...].astype(LOW)
    trade_q = Trade(net, wq_mine, lambda g: wq_back.at[g])
    wq_back[c] = wq_mine[c]
    scatter_t.total()
    table_all[c] = acc_t[...]
    share_t = [
        net.send(table_all.at[c], table_all.at[c], ctx=lax.rem(c + step, net.ctx))
        for step in range(1, net.ctx)
    ]
    scatter_o.total()
    room = acc_o.shape[1] // net.ctx
    wo_mine[...] = jnp.zeros_like(wo_mine)
    for r in range(net.ctx):
        wo_mine[r, :, :room] = acc_o[:, r * room : (r + 1) * room].astype(LOW)
    trade_o = Trade(net, wo_mine, lambda g: wo_back.at[g])
    wo_back[c] = wo_mine[c]
    trades = (trade_up, trade_down, trade_q, trade_o)
    for item in trades:
        item.received()
    for copy in share_t:
        copy.wait_recv()
    total = table_all[0]
    for other in range(1, net.ctx):
        total = total + table_all[other]
    totals[...] = total
    for item in (fold, scatter_q, scatter_o, scatter_t, *trades):
        item.finish()
    for copy in share_t:
        copy.wait_send()


def pairs_of(ref, i):
    return jnp.concatenate([ref[2 * i], ref[2 * i + 1]], axis=1)


def causal(scores, first):
    rows = lax.broadcasted_iota(jnp.int32, scores.shape, 0) + first
    columns = lax.broadcasted_iota(jnp.int32, scores.shape, 1)
    return jnp.where(columns <= rows, scores, MASKED)


def attend_kernel(
    starts,
    x_all, cot_ref, wq_ref, head_bias, head_pick, mixed_pick, wo_ref, vec_ref, up_bias_ref,
    x_ref, up_ref, down_ref,
    cot_all, normed_one, heads, lse, mixed, mixed_slots, up_all, down_all, normed_all, residual_ref,
    hidden, slope, down_grad,
    projected, flat_mixed, wide_grad, parts, near, held, far, send_sem, recv_sem,
):
    net = Net(send_sem, recv_sem)
    d, c = net.d, net.c
    up_all[d] = up_ref[...]
    down_all[d] = down_ref[...]
    cot_all[c] = cot_ref[...]
    net.greet()
    ff = down_all.shape[2]
    cut = pair_cut(ff)
    share_cot = Share(net, cot_all)
    gather_up = Gather(net, lambda z: up_all.at[net.at(z)])
    pair_down = PairGather(
        net, down_all.at[d, :, pl.ds(0, cut)], lambda z: down_all.at[pl.ds(z * 2, 2), :, pl.ds(0, cut)]
    )
    ctx, rows, width = x_all.shape
    slot = wq_ref.shape[2]
    most = mixed.shape[0]
    factor = float(HEAD_DIM) ** (-0.5)

    def norm_block(b, carry):
        scaled, _ = norm_stats(x_all[b].astype(F32))
        normed_one[b] = (scaled * vec_ref[0:1] + vec_ref[1:2]).astype(LOW)
        return carry

    lax.fori_loop(0, ctx, norm_block, 0)
    slot_bias = plain(head_bias[...], head_pick[...])[0:1]
    for i in range(net.dp // 2):
        weight = pairs_of(wq_ref, i)
        span = pl.ds(i * 2 * slot, 2 * slot)
        bias = slot_bias[:, i * 2 * slot : (i + 1) * 2 * slot]

        def project(b, carry):
            out = plain(normed_one[b], weight) + bias
            projected[b, :, span] = out.astype(LOW)
            return carry

        lax.fori_loop(0, ctx, project, 0)
    share_cot.forward()
    gather_up.step(0)
    pair_down.begin()

    def pick_block(b, carry):
        span = pl.ds(pl.multiple_of(b * rows, rows), rows)
        picked = outer_cols(projected[b], head_pick[...]).astype(LOW)
        for h in range(3 * most):
            heads[h, span] = picked[:, h * HEAD_DIM : (h + 1) * HEAD_DIM]
        return carry

    lax.fori_loop(0, ctx, pick_block, 0)

    def attend(i, carry):
        for b in range(ctx):
            here = slice(b * rows, (b + 1) * rows)
            past = slice(0, (b + 1) * rows)
            scores = outer_cols(heads[i, here], heads[most + i, past]) * factor
            scores = causal(scores, b * rows)
            peak = jnp.max(scores, axis=-1, keepdims=True)
            log_total = peak + jnp.log(jnp.sum(jnp.exp(scores - peak), axis=-1, keepdims=True))
            soft = jnp.exp(scores - log_total).astype(LOW)
            lse[i, here] = log_total
            mixed[i, here] = plain(soft, heads[2 * most + i, past]).astype(LOW)
        return carry

    lax.fori_loop(0, most, attend, 0)
    gather_up.step(1)
    pair_down.step(0)
    gather_down = Gather(net, lambda z: down_all.at[net.at(z), :, pl.ds(cut, ff - cut)])
    share_cot.finish()

    def out_block(b):
        span = pl.ds(pl.multiple_of(b * rows, rows), rows)
        for i in range(most):
            flat_mixed[:, i * HEAD_DIM : (i + 1) * HEAD_DIM] = mixed[i, span]
        mixed_slots[b] = plain(flat_mixed[...], mixed_pick[...]).astype(LOW)
        parts[b] = outer_cols(mixed_slots[b], wo_ref[...]).astype(LOW)

    fold = Fold(net, parts, near, held, far, out_block)
    for k in range(2, net.outer - 1):
        gather_up.step(k)
    fold.total(residual_ref)
    residual = x_ref[...].astype(F32) + (residual_ref[...] + vec_ref[starts[3] : starts[3] + 1])
    residual_ref[...] = residual
    scaled, _ = norm_stats(residual)
    gain, shift = vec_ref[starts[4] : starts[4] + 1], vec_ref[starts[5] : starts[5] + 1]
    normed_all[c] = (scaled * gain + shift).astype(LOW)
    share = Share(net, normed_all)
    gather_down.step(0)
    share.forward()
    pair_down.step(1)
    gather_down.step(1)
    share.finish()
    gather_up.finish()
    up_bias = up_bias_ref[pl.ds(c, 1)]
    up_flat = up_all[...].reshape(ff, width)

    def hidden_block(b, carry):
        pre = outer_cols(normed_all[b], up_flat) + up_bias
        bell = 0.5 * (1.0 + lax.erf(pre * INV_ROOT_TWO))
        hidden[pl.ds(pl.multiple_of(b * rows, rows), rows)] = (pre * bell).astype(LOW)
        slope[b] = bell + pre * jnp.exp(-0.5 * pre * pre) * INV_ROOT_TWO_PI
        return carry

    lax.fori_loop(0, ctx, hidden_block, 0)
    for k in range(2, net.outer - 1):
        gather_down.step(k)
        pair_down.step(k)
    part = down_grad.shape[1]
    cross(cot_all[...].reshape(ctx * rows, width), hidden[...], wide_grad)
    for p in range(net.dp):
        down_grad[p] = wide_grad[p * part : (p + 1) * part].astype(LOW)
    for item in (fold, gather_down, pair_down):
        item.finish()


def cross(left, right, out):
    for at in range(0, left.shape[1], 256):
        end = min(at + 256, left.shape[1])
        out[at:end] = inner_rows(left[:, at:end], right)


def return_kernel(
    starts,
    hidden, slope, down_grad,
    normed_ref, cot_all, up_flat, down_flat, residual_ref, cot_ref, vec_ref,
    wq_ref, head_pick, mixed_pick, wo_ref, normed_one, heads, lse, mixed, mixed_slots,
    block_out, grad_residual, lines, down_mine, up_mine, one_part, wq_grad, wo_grad, bias_sums,
    grad_hidden, up_total, wide_grad, up_grad, parts,
    low_all, sums, near, held, far, near_down, passed_down, near_up, passed_up, acc_down, acc_up,
    mixed_grad, grad_heads, flat_heads, grad_slots, key_total, value_total, send_sem, recv_sem,
):
    net = Net(send_sem, recv_sem)
    c = net.c
    net.greet()
    scatter_down = Scatter(net, lambda z, x: down_grad.at[z * 2 + x], near_down, passed_down, acc_down)
    ctx, rows, _ = normed_ref.shape
    part = down_grad.shape[1]
    piece = up_grad.shape[1]
    tokens = ctx * rows

    def spanned(b):
        return pl.ds(pl.multiple_of(b * rows, rows), rows)

    up_total[...] = jnp.zeros_like(up_total)

    def back_block(b):
        parts[b, :rows] = outer_cols(hidden[spanned(b)], down_flat[...]).astype(LOW)
        grad = plain(cot_all[b], down_flat[...]) * slope[b]
        low = grad.astype(LOW)
        grad_hidden[spanned(b)] = low
        parts[b, rows:] = plain(low, up_flat[...]).astype(LOW)
        up_total[...] += jnp.sum(grad, axis=0, keepdims=True)

    fold = Fold(net, parts, near, held, far, back_block)
    up_sum = up_total[...]
    scatter_down.step(0)
    normed_two = normed_ref[...].reshape(tokens, normed_ref.shape[2])
    grad_low = grad_hidden[...]
    cross(grad_low, normed_two, wide_grad)
    for p in range(net.dp):
        up_grad[p] = wide_grad[p * piece : (p + 1) * piece].astype(LOW)
    scatter_up = Scatter(net, lambda z, x: up_grad.at[z * 2 + x], near_up, passed_up, acc_up)
    fold.total(sums)
    residual = residual_ref[...]
    down_bias = vec_ref[starts[7] : starts[7] + 1]
    gain = vec_ref[starts[4] : starts[4] + 1]
    block_out[...] = (residual + (sums[pl.ds(0, rows)] + down_bias)).astype(LOW)
    scaled, inverse = norm_stats(residual)
    upstream = sums[pl.ds(rows, rows)]
    own_cot = cot_ref[...].astype(F32)
    total = own_cot + norm_backward(upstream, scaled, inverse, gain)
    grad_residual[...] = total
    low_all[c] = total.astype(LOW)
    share = Share(net, low_all)

    def line(value):
        return jnp.sum(value, axis=0, keepdims=True)

    lines[...] = jnp.zeros_like(lines)
    lines[starts[3] : starts[3] + 1] = line(total)
    lines[starts[4] : starts[4] + 1] = line(upstream * scaled)
    lines[starts[5] : starts[5] + 1] = line(upstream)
    for p in range(net.dp):
        span = slice(p * part, (p + 1) * part)
        lines[pl.ds(starts[6] + c, 1), span] = up_sum[:, p * piece : p * piece + part]
    lines[starts[7] : starts[7] + 1] = line(own_cot)
    for k in range(1, net.outer - 2):
        scatter_down.step(k)
    share.forward()
    share.finish()
    scatter_down.step(net.outer - 2)
    most = mixed.shape[0]
    slot = wq_ref.shape[2]
    factor = float(HEAD_DIM) ** (-0.5)

    def mixed_block(b, carry):
        slots = plain(low_all[b], wo_ref[...]).astype(LOW)
        picked = outer_cols(slots, mixed_pick[...]).astype(LOW)
        for i in range(most):
            mixed_grad[i, spanned(b)] = picked[:, i * HEAD_DIM : (i + 1) * HEAD_DIM]
        return carry

    lax.fori_loop(0, ctx, mixed_block, 0)

    def attend_back(i, carry):
        query_sum = jnp.zeros((1, HEAD_DIM), F32)
        for b in range(ctx - 1, -1, -1):
            here = slice(b * rows, (b + 1) * rows)
            past = slice(0, (b + 1) * rows)
            query, key, value = heads[i, here], heads[most + i, past], heads[2 * most + i, past]
            scores = causal(outer_cols(query, key) * factor, b * rows)
            probs = jnp.exp(scores - lse[i, here])
            upper = mixed_grad[i, here]
            delta = jnp.sum(upper.astype(F32) * mixed[i, here].astype(F32), axis=-1, keepdims=True)
            grad_scores = (probs * (outer_cols(upper, value) - delta) * factor).astype(LOW)
            grad_query = plain(grad_scores, key)
            query_sum = query_sum + jnp.sum(grad_query, axis=0, keepdims=True)
            grad_heads[i, here] = grad_query.astype(LOW)
            key_part = inner_rows(grad_scores, query)
            value_part = inner_rows(probs.astype(LOW), upper)
            if b == ctx - 1:
                key_total[...] = key_part
                value_total[...] = value_part
            else:
                key_total[past] += key_part
                value_total[past] += value_part
        grad_heads[most + i] = key_total[...].astype(LOW)
        grad_heads[2 * most + i] = value_total[...].astype(LOW)
        bias_sums[i] = query_sum
        bias_sums[most + i] = jnp.sum(value_total[...], axis=0, keepdims=True)
        return carry

    lax.fori_loop(0, 2, attend_back, 0)
    scatter_up.step(0)
    lax.fori_loop(2, most, attend_back, 0)
    for k in range(1, net.outer - 2):
        scatter_up.step(k)

    def slot_block(b, carry):
        span = spanned(b)
        for h in range(3 * most):
            flat_heads[:, h * HEAD_DIM : (h + 1) * HEAD_DIM] = grad_heads[h, span]
        grad_slots[span] = plain(flat_heads[...], head_pick[...]).astype(LOW)
        total = outer_cols(grad_slots[span, : 2 * slot], pairs_of(wq_ref, 0))
        for i in range(1, net.dp // 2):
            part = grad_slots[span, i * 2 * slot : (i + 1) * 2 * slot]
            total = total + outer_cols(part, pairs_of(wq_ref, i))
        one_part[b] = total.astype(LOW)
        return carry

    lax.fori_loop(0, ctx, slot_block, 0)
    scatter_up.step(net.outer - 2)
    normed = normed_one[...]
    for i in range(net.dp // 2):
        weight_grad = inner_rows(normed, grad_slots[:, i * 2 * slot : (i + 1) * 2 * slot])
        wq_grad[2 * i] = weight_grad[:, :slot].astype(LOW)
        wq_grad[2 * i + 1] = weight_grad[:, slot:].astype(LOW)
    weight_grad = inner_rows(low_all[0], mixed_slots[0])
    for b in range(1, ctx):
        weight_grad = weight_grad + inner_rows(low_all[b], mixed_slots[b])
    wo_grad[...] = weight_grad.astype(LOW)
    scatter_down.total()
    down_mine[...] = acc_down[...].astype(LOW)
    scatter_up.total()
    up_mine[...] = acc_up[...].astype(LOW)
    for item in (fold, scatter_down, scatter_up):
        item.finish()


def pair_cut(lanes):
    return rounded_up(lanes // 3, 128)


def attention(x_flat, gain, shift, wq, bias_slots, head_pick, mixed_pick, wo, most):
    tokens = x_flat.shape[0]
    factor = float(HEAD_DIM) ** (-0.5)
    scaled, _ = norm_stats(x_flat.astype(F32))
    normed = (scaled * gain + shift).astype(LOW)
    projected = jnp.einsum("tk,dks->tds", normed, wq, preferred_element_type=F32)
    projected = (projected.reshape(tokens, -1) + bias_slots).astype(LOW)
    heads = outer_cols(projected, head_pick).astype(LOW)
    heads = heads.reshape(tokens, 3, most, HEAD_DIM).transpose(1, 2, 0, 3)
    queries, keys, values = heads[0], heads[1], heads[2]
    index = jnp.arange(tokens, dtype=jnp.int32)
    scores = jnp.einsum("hqd,hkd->hqk", queries, keys, preferred_element_type=F32) * factor
    scores = jnp.where(index[None, :] <= index[:, None], scores, MASKED)
    peak = jnp.max(scores, axis=-1, keepdims=True)
    log_total = peak + jnp.log(jnp.sum(jnp.exp(scores - peak), axis=-1, keepdims=True))
    probs = jnp.exp(scores - log_total)
    soft = probs.astype(LOW)
    mixed = jnp.einsum("hqk,hkd->hqd", soft, values, preferred_element_type=F32).astype(LOW)
    mixed_flat = mixed.transpose(1, 0, 2).reshape(tokens, most * HEAD_DIM)
    mixed_slots = plain(mixed_flat, mixed_pick).astype(LOW)
    out_part = outer_cols(mixed_slots, wo).astype(LOW)
    return normed, queries, keys, values, probs, soft, mixed, mixed_slots, out_part


def attention_back(
    low, normed, queries, keys, values, probs, soft, mixed, mixed_slots, wq, wo, head_pick, mixed_pick
):
    most, tokens = mixed.shape[:2]
    dp, _, slot = wq.shape
    factor = float(HEAD_DIM) ** (-0.5)
    grad_mixed = outer_cols(plain(low, wo).astype(LOW), mixed_pick).astype(LOW)
    grad_mixed = grad_mixed.reshape(tokens, most, HEAD_DIM).transpose(1, 0, 2)
    grad_probs = jnp.einsum("hqd,hkd->hqk", grad_mixed, values, preferred_element_type=F32)
    delta = jnp.sum(grad_mixed.astype(F32) * mixed.astype(F32), axis=-1, keepdims=True)
    grad_scores = (probs * (grad_probs - delta) * factor).astype(LOW)
    grad_q = jnp.einsum("hqk,hkd->hqd", grad_scores, keys, preferred_element_type=F32)
    grad_k = jnp.einsum("hqk,hqd->hkd", grad_scores, queries, preferred_element_type=F32)
    grad_v = jnp.einsum("hqk,hqd->hkd", soft, grad_mixed, preferred_element_type=F32)
    bias_sums = jnp.sum(jnp.stack([grad_q, grad_v]), axis=2)
    grad_heads = jnp.stack([grad_q, grad_k, grad_v]).astype(LOW)
    grad_heads = grad_heads.transpose(2, 0, 1, 3).reshape(tokens, 3 * most * HEAD_DIM)
    grad_slots = plain(grad_heads, head_pick).astype(LOW).reshape(tokens, dp, slot)
    one_part = jnp.einsum("tds,dks->tk", grad_slots, wq, preferred_element_type=F32).astype(LOW)
    wq_grad = jnp.einsum("tk,tds->dks", normed, grad_slots, preferred_element_type=F32).astype(LOW)
    wo_grad = inner_rows(low, mixed_slots).astype(LOW)
    return one_part, wq_grad, wo_grad, bias_sums


def on_device(
    block_input,
    norm_one_gain,
    norm_one_bias,
    w_qkv,
    bias_qv,
    w_out,
    bias_out,
    norm_two_gain,
    norm_two_bias,
    w_up,
    bias_up,
    w_down,
    bias_down,
    cotangent,
):
    seq_count, block_len, width = block_input.shape
    rows = seq_count * block_len
    ctx = lax.axis_size("ctx")
    dp = lax.axis_size("dp")
    d, c = lax.axis_index("dp"), lax.axis_index("ctx")
    fold = dp // ctx
    outer = dp // 2
    tokens = rows * ctx
    grad_scale = float(tokens * dp) ** (-0.5)
    factor = float(HEAD_DIM) ** (-0.5)
    high, wide = w_qkv.shape
    part = w_out.shape[1]
    units = w_up.shape[1]
    share_units = units // ctx

    tables = slot_tables(width, dp, ctx)
    most, slot, row_slot = tables["most"], tables["slot"], tables["row_slot"]
    mixed_wide = ctx * tables["row_pack"]

    column_pick = picker(tables["column_pick"], d, wide)
    row_pick = picker(tables["row_pick"], c, high)

    wq = plain(w_qkv, column_pick).astype(LOW).reshape(high, ctx, slot).transpose(1, 0, 2)
    wo = inner_rows(w_out, row_pick).astype(LOW).reshape(part, ctx, row_slot).transpose(1, 0, 2)
    up = w_up.T.reshape(ctx, share_units, high)
    down = (
        w_down.reshape(fold, ctx, share_units, part)
        .transpose(1, 3, 0, 2)
        .reshape(ctx, part, fold * share_units)
    )
    pieces = (
        norm_one_gain,
        norm_one_bias,
        bias_qv,
        bias_out,
        norm_two_gain,
        norm_two_bias,
        bias_up,
        bias_down,
    )
    lines = [v.shape[0] // part for v in pieces]
    line_count = sum(lines)
    line_room = rounded_up(line_count, 16)
    *pieces, wq, wo, up, down = lax.optimization_barrier((*pieces, wq, wo, up, down))
    vec = jnp.concatenate([*pieces, jnp.zeros(((line_room - line_count) * part,), LOW)])
    vec = vec.reshape(line_room, part)

    x_own = block_input.reshape(rows, width)
    cot_own = cotangent.reshape(rows, width)

    fused = dp * slot <= 2048
    x_all, wq_all, up_mine, down_mine, vec_all, wo_all, *more = net_call(
        functools.partial(first_kernel, fused),
        0,
        "gather_first",
        (x_own, cot_own, wq, wo, up, down, vec),
        [
            ((ctx, rows, width), LOW),
            ((dp, ctx, high, slot), LOW),
            (up.shape, LOW),
            (down.shape, LOW),
            ((dp, line_room, part), LOW),
            ((dp, part, mixed_wide), LOW),
            *([] if fused else [((ctx, rows, width), LOW)]),
        ],
        scratch=[pltpu.VMEM((ctx, part, row_slot), LOW)],
        copies=12 * outer + 64,
    )

    room = rounded_up(share_units, 16)
    extra = room - share_units
    ff = dp * room
    ups = jnp.pad(up_mine.transpose(1, 0, 2).reshape(share_units, width), ((0, extra), (0, 0)))
    downs = down_mine.transpose(1, 0, 2).reshape(part, dp, share_units)
    downs = jnp.pad(downs, ((0, 0), (0, 0), (0, extra))).reshape(part, ff)

    across = vec_all.transpose(1, 0, 2).reshape(line_room, width).astype(F32)
    starts = np.cumsum([0] + lines)
    starts = [int(v) for v in starts]
    up_bias = jnp.pad(vec_all[:, starts[6] : starts[7]], ((0, 0), (0, 0), (0, extra)))
    up_bias = up_bias.transpose(1, 0, 2).reshape(ctx, ff).astype(F32)
    bias_q_v = vec_all[:, starts[2] : starts[3]].reshape(2, HEADS, HEAD_DIM)

    head_rows = lax.dynamic_index_in_dim(jnp.asarray(tables["head_rows"]), c, 0, keepdims=False)
    head_hot = head_rows[:, None] == jnp.arange(HEADS, dtype=jnp.int32)[None, :]
    bias_heads = jnp.einsum("ih,thf->tif", head_hot.astype(LOW), bias_q_v, preferred_element_type=F32)
    bias_heads = jnp.concatenate(
        [bias_heads[:1], jnp.zeros_like(bias_heads[:1]), bias_heads[1:]]
    ).reshape(1, -1)

    wq_flat = wq_all.reshape(dp, width, slot)
    head_pick = row_picker(tables["head_pick"], c, dp * slot)
    mixed_pick = row_picker(tables["mixed_pick"], c, mixed_wide)
    wo_flat = wo_all.reshape(width, mixed_wide)
    if fused:
        (
            cot_all, normed_one, heads, lse, mixed, mixed_slots, up_all, down_all, normed_two,
            residual, hidden, slope, down_grad,
        ) = net_call(
            functools.partial(attend_kernel, starts),
            1,
            "attend_second",
            (
                x_all, cot_own, wq_flat, jnp.tile(bias_heads.astype(LOW), (16, 1)), head_pick,
                mixed_pick, wo_flat, across, up_bias, x_own, ups, downs,
            ),
            [
                ((ctx, rows, width), LOW),
                ((ctx, rows, width), LOW),
                ((3 * most, tokens, HEAD_DIM), LOW),
                ((most, tokens, 1), F32),
                ((most, tokens, HEAD_DIM), LOW),
                ((ctx, rows, mixed_wide), LOW),
                ((dp, room, width), LOW),
                ((dp, part, ff), LOW),
                ((ctx, rows, width), LOW),
                ((rows, width), F32),
                ((tokens, ff), LOW),
                ((ctx, rows, ff), F32),
                ((dp, part, ff), LOW),
            ],
            scratch=[
                pltpu.VMEM((ctx, rows, dp * slot), LOW),
                pltpu.VMEM((rows, most * HEAD_DIM), LOW),
                pltpu.VMEM((width, ff), F32),
                pltpu.VMEM((ctx, rows, width), LOW),
                *fold_scratch(rows, width),
            ],
            copies=18 * outer + 64,
        )
    else:
        cot_all = more[0]
        normed_one, queries, keys, values, probs, soft_weights, mixed, mixed_slots, out_part = attention(
            x_all.reshape(tokens, width), across[0:1], across[1:2], wq_flat,
            plain(bias_heads.astype(LOW), head_pick), head_pick, mixed_pick, wo_flat, most,
        )
        up_all, down_all, normed_two, residual = net_call(
            second_kernel,
            1,
            "gather_second",
            (
                out_part.reshape(ctx, rows, width), x_own, ups, downs,
                *[across[starts[i] : starts[i] + 1] for i in (3, 4, 5)],
            ),
            [
                ((dp, room, width), LOW),
                ((dp, part, ff), LOW),
                ((ctx, rows, width), LOW),
                ((rows, width), F32),
            ],
            scratch=fold_scratch(rows, width),
            copies=12 * outer + 64,
        )
    up_flat = up_all.reshape(ff, width)
    down_flat = down_all.reshape(width, ff)
    third_scratch = [
        pltpu.VMEM((2 * rows, width), F32),
        *fold_scratch(2 * rows, width),
        pltpu.VMEM((outer, part, ff), LOW),
        pltpu.VMEM((outer + 1, part, ff), LOW),
        pltpu.VMEM((outer, room, width), LOW),
        pltpu.VMEM((outer + 1, room, width), LOW),
        pltpu.VMEM((part, ff), F32),
        pltpu.VMEM((room, width), F32),
    ]
    third_sums = [((part, ff), LOW), ((room, width), LOW)]
    if fused:
        (
            block_output, grad_residual, small, down_sum, up_sum,
            one_part, wq_grad, wo_grad, bias_sums,
        ) = net_call(
            functools.partial(return_kernel, starts),
            2,
            "return_third",
            (
                hidden, slope, down_grad,
                normed_two, cot_all, up_flat, down_flat, residual, cot_own, across,
                wq_flat, head_pick, mixed_pick, wo_flat,
                normed_one.reshape(tokens, width), heads, lse, mixed, mixed_slots,
            ),
            [
                ((rows, width), LOW),
                ((rows, width), F32),
                ((line_room, width), F32),
                *third_sums,
                ((ctx, rows, width), LOW),
                ((dp, width, slot), LOW),
                ((width, mixed_wide), LOW),
                ((2 * most, 1, HEAD_DIM), F32),
            ],
            scratch=[
                pltpu.VMEM((tokens, ff), LOW),
                pltpu.VMEM((1, ff), F32),
                pltpu.VMEM((ff, width), F32),
                pltpu.VMEM((dp, room, width), LOW),
                pltpu.VMEM((ctx, 2 * rows, width), LOW),
                pltpu.VMEM((ctx, rows, width), LOW),
                *third_scratch,
                pltpu.VMEM((most, tokens, HEAD_DIM), LOW),
                pltpu.VMEM((3 * most, tokens, HEAD_DIM), LOW),
                pltpu.VMEM((rows, 3 * most * HEAD_DIM), LOW),
                pltpu.VMEM((tokens, dp * slot), LOW),
                pltpu.VMEM((tokens, HEAD_DIM), F32),
                pltpu.VMEM((tokens, HEAD_DIM), F32),
            ],
            copies=6 * outer + 64,
        )
        bias_sums = bias_sums.reshape(2, most, HEAD_DIM)
    else:
        normed_two = normed_two.reshape(tokens, width)
        cot_flat = cot_all.reshape(tokens, width)
        hidden_pre = outer_cols(normed_two, up_flat) + lax.dynamic_slice_in_dim(up_bias, c, 1, axis=0)
        hidden = gelu_value(hidden_pre).astype(LOW)
        down_part = outer_cols(hidden, down_flat).astype(LOW).reshape(ctx, rows, width)
        grad_hidden = plain(cot_flat, down_flat) * gelu_slope(hidden_pre)
        grad_hidden_low = grad_hidden.astype(LOW)
        normed_part = plain(grad_hidden_low, up_flat).astype(LOW).reshape(ctx, rows, width)
        down_grad = inner_rows(cot_flat, hidden).astype(LOW).reshape(dp, part, ff)
        up_grad = inner_rows(grad_hidden_low, normed_two).astype(LOW).reshape(dp, room, width)
        block_output, grad_residual, grad_normed_two, low_all, down_sum, up_sum = net_call(
            third_kernel,
            2,
            "scatter_third",
            (
                jnp.concatenate([down_part, normed_part], axis=1),
                residual,
                cot_own,
                down_grad,
                up_grad,
                across[starts[7] : starts[7] + 1],
                across[starts[4] : starts[4] + 1],
            ),
            [
                ((rows, width), LOW),
                ((rows, width), F32),
                ((rows, width), F32),
                ((ctx, rows, width), LOW),
                *third_sums,
            ],
            scratch=third_scratch,
            copies=6 * outer + 64,
        )
        one_part, wq_grad, wo_grad, bias_sums = attention_back(
            low_all.reshape(tokens, width), normed_one, queries, keys, values, probs, soft_weights,
            mixed, mixed_slots, wq_flat, wo_flat, head_pick, mixed_pick,
        )
        one_part = one_part.reshape(ctx, rows, width)
        scaled_two, _ = norm_stats(residual)
        up_lines = jnp.where(
            jnp.arange(ctx, dtype=jnp.int32)[:, None] == c,
            jnp.sum(grad_hidden, axis=0).reshape(dp, room)[:, :share_units].reshape(1, width),
            0.0,
        )
        small = jnp.concatenate(
            [
                jnp.zeros((starts[3], width), F32),
                jnp.sum(grad_residual, axis=0)[None],
                jnp.sum(grad_normed_two * scaled_two, axis=0)[None],
                jnp.sum(grad_normed_two, axis=0)[None],
                up_lines,
                jnp.sum(cot_own.astype(F32), axis=0)[None],
                jnp.zeros((line_room - line_count, width), F32),
            ]
        )
    wq_grad = wq_grad.reshape(dp, ctx, high, slot)
    wo_grad = wo_grad.reshape(dp, part, mixed_wide)

    bias_grad = jnp.einsum(
        "ih,tif->thf", head_hot.astype(F32), bias_sums, precision=lax.Precision.HIGHEST
    )
    bias_lines = bias_grad.reshape(dp, -1, part).transpose(1, 0, 2).reshape(-1, width)
    back_up = up_sum[:share_units].reshape(share_units, ctx, high).transpose(1, 0, 2)
    back_down = down_sum.T.reshape(dp, room, part)[:, :share_units]
    back_down = back_down.reshape(ctx, fold * share_units, part)

    grad_input, wq_back, wo_back, totals, up_back, down_back = net_call(
        last_kernel,
        3,
        "scatter_last",
        (
            one_part, wq_grad, wo_grad, small, bias_lines, back_up, back_down, x_own, grad_residual,
            across[0:1],
        ),
        [
            ((rows, width), F32),
            ((ctx, high, slot), LOW),
            ((ctx, part, row_slot), LOW),
            ((line_room, part), F32),
            (back_up.shape, LOW),
            (back_down.shape, LOW),
        ],
        scratch=[
            pltpu.VMEM((rows, width), F32),
            *fold_scratch(rows, width),
            *[pltpu.VMEM((outer + i, ctx, high, slot), LOW) for i in (0, 1)],
            *[pltpu.VMEM((outer + i, part, mixed_wide), LOW) for i in (0, 1)],
            *[pltpu.VMEM((outer + i, line_room, part), F32) for i in (0, 1)],
            pltpu.VMEM((ctx, high, slot), F32),
            pltpu.VMEM((part, mixed_wide), F32),
            pltpu.VMEM((line_room, part), F32),
            pltpu.VMEM((ctx, high, slot), LOW),
            pltpu.VMEM((ctx, part, row_slot), LOW),
            pltpu.VMEM((line_room, width), F32),
            pltpu.VMEM((dp, line_room, part), F32),
            pltpu.VMEM((ctx, line_room, part), F32),
        ],
        copies=9 * outer + 64,
    )
    wq_rows = wq_back.transpose(1, 0, 2).reshape(high, ctx * slot)
    grad_qkv = outer_cols(wq_rows, column_pick) * grad_scale
    wo_rows = wo_back.transpose(1, 0, 2).reshape(part, ctx * row_slot)
    grad_out = outer_cols(row_pick, wo_rows) * grad_scale
    grad_up = up_back.reshape(units, high).T.astype(F32) * grad_scale
    grad_down = (
        down_back.reshape(ctx, fold, share_units, part)
        .transpose(1, 0, 2, 3)
        .reshape(w_down.shape)
        .astype(F32)
        * grad_scale
    )
    totals = totals * grad_scale
    owned = [totals[starts[i] : starts[i + 1]].reshape(-1) for i in range(len(lines))]
    return (
        block_input_like(block_output, seq_count, block_len),
        block_input_like(grad_input, seq_count, block_len),
        owned[0],
        owned[1],
        grad_qkv,
        owned[2],
        grad_out,
        owned[3],
        owned[4],
        owned[5],
        grad_up,
        owned[6],
        grad_down,
        owned[7],
    )


def block_input_like(flat, seq_count, block_len):
    return flat.reshape(seq_count, block_len, flat.shape[-1])


def solution(mesh):
    in_specs = (
        P("dp", "ctx", None),
        P("dp"),
        P("dp"),
        P("ctx", "dp"),
        P("dp"),
        P("ctx", "dp"),
        P("dp"),
        P("dp"),
        P("dp"),
        P("ctx", "dp"),
        P("dp"),
        P("ctx", "dp"),
        P("dp"),
        P("dp", "ctx", None),
    )
    out_specs = (
        P("dp", "ctx", None),
        P("dp", "ctx", None),
        P("dp"),
        P("dp"),
        P("ctx", "dp"),
        P("dp"),
        P("ctx", "dp"),
        P("dp"),
        P("dp"),
        P("dp"),
        P("ctx", "dp"),
        P("dp"),
        P("ctx", "dp"),
        P("dp"),
    )
    return jax.shard_map(
        on_device, mesh=mesh, in_specs=in_specs, out_specs=out_specs, check_vma=False
    )
```

```python
import functools

import jax
import jax.numpy as jnp
import numpy as np
from jax import lax
from jax.experimental import pallas as pl
from jax.experimental.pallas import tpu as pltpu
from jax.sharding import PartitionSpec as P

HEADS = 17
HEAD_DIM = 64
HEAD_GROUP = (0, 2, 1, 3, 2, 0, 1, 3, 0, 1, 2, 0, 3, 3, 2, 0, 1)

EPS = 1e-05
MASKED = -1e30
INV_ROOT_TWO = 0.7071067811865476
INV_ROOT_TWO_PI = 0.3989422804014327

F32 = jnp.float32
LOW = jnp.bfloat16
VMEM_LIMIT = 60 * 1024 * 1024


def norm_stats(rows_in):
    center = jnp.mean(rows_in, axis=-1, keepdims=True)
    offset = rows_in - center
    spread = jnp.mean(offset * offset, axis=-1, keepdims=True)
    inverse = lax.rsqrt(spread + EPS)
    return offset * inverse, inverse


def norm_backward(upstream, scaled, inverse, gain):
    weighted = upstream * gain
    first = jnp.mean(weighted, axis=-1, keepdims=True)
    second = jnp.mean(weighted * scaled, axis=-1, keepdims=True)
    return inverse * (weighted - first - scaled * second)


def gelu_value(pre):
    return 0.5 * pre * (1.0 + lax.erf(pre * INV_ROOT_TWO))


def gelu_slope(pre):
    return (
        0.5 * (1.0 + lax.erf(pre * INV_ROOT_TWO))
        + pre * jnp.exp(-0.5 * pre * pre) * INV_ROOT_TWO_PI
    )


def inner_rows(left, right):
    return lax.dot_general(left, right, (((0,), (0,)), ((), ())), preferred_element_type=F32)


def outer_cols(left, right):
    return lax.dot_general(left, right, (((1,), (1,)), ((), ())), preferred_element_type=F32)


def plain(left, right):
    return jnp.dot(left, right, preferred_element_type=F32)


def rounded_up(value, step):
    return -(-value // step) * step


def slot_tables(width, dp, ctx):
    group = np.array(HEAD_GROUP)
    heads_of = [np.flatnonzero(group == g) for g in range(ctx)]
    most = max(len(h) for h in heads_of)
    head_rows = np.full((ctx, most), -1, np.int32)
    for g in range(ctx):
        head_rows[g, : len(heads_of[g])] = heads_of[g]

    wide = 3 * width // dp
    column = np.arange(3 * width)
    column_group = group[(column % width) // HEAD_DIM]
    column_dp = column // wide
    lists = [
        [column[(column_dp == d) & (column_group == g)] for g in range(ctx)] for d in range(dp)
    ]
    slot = rounded_up(max(len(v) for row in lists for v in row), 128)
    column_pick = np.full((dp, ctx * slot), -1, np.int32)
    place = np.full((3 * width,), -1, np.int32)
    for d in range(dp):
        for g in range(ctx):
            v = lists[d][g]
            column_pick[d, g * slot : g * slot + len(v)] = v - d * wide
            place[v] = d * slot + np.arange(len(v))
    head_pick = np.full((ctx, 3, most, HEAD_DIM), -1, np.int32)
    for g in range(ctx):
        for i, h in enumerate(heads_of[g]):
            for t in range(3):
                at = t * width + h * HEAD_DIM
                head_pick[g, t, i] = place[at : at + HEAD_DIM]
    head_pick = head_pick.reshape(ctx, -1)

    high = width // ctx
    row = np.arange(width)
    row_group = group[row // HEAD_DIM]
    row_lists = [[row[(row // high == r) & (row_group == g)] for g in range(ctx)] for r in range(ctx)]
    row_pack = rounded_up(max(len(v) for one in row_lists for v in one), 32)
    row_slot = rounded_up(row_pack, 128)
    row_pick = np.full((ctx, ctx * row_slot), -1, np.int32)
    row_place = np.full((width,), -1, np.int32)
    for r in range(ctx):
        for g in range(ctx):
            v = row_lists[r][g]
            row_pick[r, g * row_slot : g * row_slot + len(v)] = v - r * high
            row_place[v] = r * row_pack + np.arange(len(v))
    mixed_pick = np.full((ctx, most, HEAD_DIM), -1, np.int32)
    for g in range(ctx):
        for i, h in enumerate(heads_of[g]):
            mixed_pick[g, i] = row_place[h * HEAD_DIM : (h + 1) * HEAD_DIM]
    return dict(
        most=most,
        slot=slot,
        row_slot=row_slot,
        row_pack=row_pack,
        head_rows=head_rows,
        column_pick=column_pick,
        head_pick=head_pick,
        row_pick=row_pick,
        mixed_pick=mixed_pick.reshape(ctx, -1),
    )


def picker(table, which, size, dtype=LOW):
    chosen = lax.dynamic_index_in_dim(jnp.asarray(table), which, 0, keepdims=False)
    return (jnp.arange(size, dtype=jnp.int32)[:, None] == chosen[None, :]).astype(dtype)


def row_picker(table, which, size, dtype=LOW):
    chosen = lax.dynamic_index_in_dim(jnp.asarray(table), which, 0, keepdims=False)
    return (chosen[:, None] == jnp.arange(size, dtype=jnp.int32)[None, :]).astype(dtype)


class Net:
    def __init__(self, send_sem, recv_sem):
        self.send_sem, self.recv_sem = send_sem, recv_sem
        self.used = 0
        self.dp = lax.axis_size("dp")
        self.ctx = lax.axis_size("ctx")
        self.inner = 2
        self.outer = self.dp // self.inner
        self.d = lax.axis_index("dp")
        self.c = lax.axis_index("ctx")
        self.z = self.d // self.inner
        self.x = lax.rem(self.d, self.inner)
        self.beside = self.z * self.inner + (1 - self.x)
        self.partner = self.c + 1 - 2 * lax.rem(self.c, 2)
        self.across = lax.rem(self.c + 2, 4)
        self.corner = lax.rem(self.partner + 2, 4)

    def at(self, z):
        return z * self.inner + self.x

    def greet(self):
        barrier = pltpu.get_barrier_semaphore()
        self.signal(barrier, {"dp": self.beside})
        for step in range(1, self.ctx):
            self.signal(barrier, {"ctx": lax.rem(self.c + step, self.ctx)})

        @pl.when(self.z > 0)
        def _():
            self.signal(barrier, {"dp": self.at(self.z - 1)})

        @pl.when(self.z < self.outer - 1)
        def _():
            self.signal(barrier, {"dp": self.at(self.z + 1)})

        ends = jnp.where(self.z > 0, 1, 0) + jnp.where(self.z < self.outer - 1, 1, 0)
        pl.semaphore_wait(barrier, self.ctx + ends)

    @staticmethod
    def signal(barrier, device):
        pl.semaphore_signal(
            barrier, inc=1, device_id=device, device_id_type=pl.DeviceIdType.MESH
        )

    def room(self, count):
        at = self.used
        self.used += count
        return at

    def copy(self, at, source, dest, **device):
        return pltpu.make_async_remote_copy(
            src_ref=source,
            dst_ref=dest,
            send_sem=self.send_sem.at[at],
            recv_sem=self.recv_sem.at[at],
            device_id=device,
            device_id_type=pl.DeviceIdType.MESH,
        )

    def send(self, source, dest, **device):
        copy = self.copy(self.room(1), source, dest, **device)
        copy.start()
        return copy


class Gather:
    def __init__(self, net, place, hop=True):
        self.net, self.place, self.hop = net, place, hop
        links = net.outer - 1
        self.right, self.left = net.room(links), net.room(links)
        self.hop_right, self.hop_left = net.room(links), net.room(links)
        if hop:
            mine = place(net.z)
            self.own = net.send(mine, mine, dp=net.beside)
        self.pass_on(0, net.z, net.z < net.outer - 1, net.z > 0)

    def moving(self, base, k, z, toward):
        view = self.place(z)
        return self.net.copy(base + k, view, view, dp=self.net.at(self.net.z + toward))

    def beside(self, base, k, z):
        view = self.place(z)
        return self.net.copy(base + k, view, view, dp=self.net.beside)

    def pass_on(self, k, z, right, left):
        if k >= self.net.outer - 1:
            return
        if right is not None:

            @pl.when(right)
            def _():
                self.moving(self.right, k, z, 1).start()

        if left is not None:

            @pl.when(left)
            def _():
                self.moving(self.left, k, z, -1).start()

    def step(self, k):
        net = self.net
        from_left, from_right = net.z - 1 - k, net.z + 1 + k

        @pl.when(from_left >= 0)
        def _():
            self.moving(self.right, k, from_left, -1).wait_recv()
            self.pass_on(k + 1, from_left, net.z < net.outer - 1, None)
            if self.hop:
                self.beside(self.hop_right, k, from_left).start()

        @pl.when(from_right < net.outer)
        def _():
            self.moving(self.left, k, from_right, 1).wait_recv()
            self.pass_on(k + 1, from_right, None, net.z > 0)
            if self.hop:
                self.beside(self.hop_left, k, from_right).start()

    def finish(self):
        net = self.net
        if self.hop:
            self.own.wait()
        for k in range(net.outer - 1):
            here_left, here_right = net.z - k, net.z + k

            @pl.when((here_left >= 0) & (net.z < net.outer - 1))
            def _():
                self.moving(self.right, k, here_left, 1).wait_send()

            @pl.when((here_right < net.outer) & (net.z > 0))
            def _():
                self.moving(self.left, k, here_right, -1).wait_send()

            if self.hop:

                @pl.when(net.z - 1 - k >= 0)
                def _():
                    self.beside(self.hop_right, k, net.z - 1 - k).wait()

                @pl.when(net.z + 1 + k < net.outer)
                def _():
                    self.beside(self.hop_left, k, net.z + 1 + k).wait()


class PairGather:
    def __init__(self, net, mine, pair):
        self.net, self.pair = net, pair
        self.own = net.send(mine, mine, dp=net.beside)

    def begin(self):
        self.own.wait()
        self.chain = Gather(self.net, self.pair, hop=False)

    def step(self, k):
        self.chain.step(k)

    def finish(self):
        self.chain.finish()


class Scatter:
    def __init__(self, net, source, near, passed, acc):
        self.net, self.source, self.near, self.passed, self.acc = net, source, near, passed, acc
        self.hop = net.room(net.outer)
        self.right, self.left = net.room(net.outer), net.room(net.outer)
        for k in range(net.outer - 1):
            self.each(k, lambda flow, z: self.over(z).start())
        self.over(net.z).start()

    def each(self, k, act):
        net = self.net
        back = net.outer - 1 - net.z

        @pl.when(k >= net.z)
        def _():
            act(1, net.outer - 1 - (k - net.z))

        @pl.when(k >= back)
        def _():
            act(-1, k - back)

    def over(self, z):
        return self.net.copy(
            self.hop + z, self.source(z, 1 - self.net.x), self.near.at[z], dp=self.net.beside
        )

    def term(self, z):
        return self.source(z, self.net.x)[...].astype(F32) + self.near[z].astype(F32)

    def slot(self, flow, z, here):
        if flow > 0:
            return z
        return jnp.where(z < here, z, self.net.outer)

    def moving(self, flow, z):
        net = self.net
        base = self.right if flow > 0 else self.left
        there = net.z + flow
        return net.copy(
            base + z, self.near.at[z], self.passed.at[self.slot(flow, z, there)], dp=net.at(there)
        )

    def arrived(self, flow, z):
        net = self.net
        base = self.right if flow > 0 else self.left
        slot = self.slot(flow, z, net.z)
        net.copy(
            base + z, self.near.at[z], self.passed.at[slot], dp=net.at(net.z - flow)
        ).wait_recv()
        return slot

    def push(self, flow, z):
        net = self.net
        first = net.z == (0 if flow > 0 else net.outer - 1)
        self.over(z).wait_recv()

        @pl.when(first)
        def _():
            self.near[z] = self.term(z).astype(self.near.dtype)

        @pl.when(jnp.logical_not(first))
        def _():
            slot = self.arrived(flow, z)
            self.near[z] = (self.term(z) + self.passed[slot].astype(F32)).astype(self.near.dtype)

        self.moving(flow, z).start()

    def step(self, k):
        self.each(k, self.push)

    def total(self):
        net = self.net
        self.over(net.z).wait_recv()
        self.acc[...] = self.term(net.z)

        @pl.when(net.z > 0)
        def _():
            self.acc[...] += self.passed[self.arrived(1, net.z)].astype(F32)

        @pl.when(net.z < net.outer - 1)
        def _():
            self.acc[...] += self.passed[self.arrived(-1, net.z)].astype(F32)

    def finish(self):
        net = self.net
        self.over(net.z).wait_send()
        for z in range(net.outer):

            @pl.when(net.z != z)
            def _():
                self.over(z).wait_send()

            @pl.when(z > net.z)
            def _():
                self.moving(1, z).wait_send()

            @pl.when(z < net.z)
            def _():
                self.moving(-1, z).wait_send()


class Share:
    def __init__(self, net, whole, chunks=4):
        self.net, self.whole = net, whole
        size = whole.shape[1] // chunks
        self.spans = [pl.ds(part * size, size) for part in range(chunks)]
        self.far = [self.send(net.c, s, net.across) for s in self.spans]
        self.near = [self.send(net.c, s, net.partner) for s in self.spans]
        self.handed = []

    def send(self, slot, span, target):
        view = self.whole.at[slot, span]
        return self.net.send(view, view, ctx=target)

    def forward(self):
        for part, s in enumerate(self.spans):
            self.far[part].wait_recv()
            self.handed.append(self.send(self.net.across, s, self.net.partner))

    def finish(self):
        for part in range(len(self.spans)):
            self.far[part].wait_send()
            self.near[part].wait()
            self.handed[part].wait()


class Fold:
    def __init__(self, net, parts, near, held, far, make=None, chunks=4):
        self.net, self.parts, self.near, self.held, self.far_in = net, parts, near, held, far
        size = parts.shape[1] // chunks
        self.spans = [pl.ds(part * size, size) for part in range(chunks)]
        make = make or (lambda owner: None)
        make(net.corner)
        self.first = [
            net.send(parts.at[net.corner, s], near.at[0, s], ctx=net.partner) for s in self.spans
        ]
        make(net.across)
        self.far = []
        for part, s in enumerate(self.spans):
            self.first[part].wait_recv()
            self.held[s] = (
                self.parts[net.across, s].astype(F32) + self.near[0, s].astype(F32)
            ).astype(LOW)
            self.far.append(net.send(self.held.at[s], self.far_in.at[s], ctx=net.across))
        make(net.partner)
        self.own = [
            net.send(parts.at[net.partner, s], near.at[1, s], ctx=net.partner) for s in self.spans
        ]
        make(net.c)

    def total(self, out):
        net = self.net
        for part, s in enumerate(self.spans):
            self.own[part].wait_recv()
            out[s] = self.parts[net.c, s].astype(F32) + self.near[1, s].astype(F32)
        for part, s in enumerate(self.spans):
            self.far[part].wait_recv()
            out[s] = out[s] + self.far_in[s].astype(F32)

    def finish(self):
        for part in range(len(self.spans)):
            self.first[part].wait_send()
            self.own[part].wait_send()
            self.far[part].wait_send()


class Trade:
    def __init__(self, net, block, place):
        self.copies = []
        for step in (2, 1, 3):
            target = lax.rem(net.c + step, net.ctx)
            self.copies.append(net.send(block.at[target], place(net.c), ctx=target))

    def received(self):
        for copy in self.copies:
            copy.wait_recv()

    def finish(self):
        for copy in self.copies:
            copy.wait_send()


def fold_scratch(rows, wide):
    return [
        pltpu.VMEM((2, rows, wide), LOW),
        pltpu.VMEM((rows, wide), LOW),
        pltpu.VMEM((rows, wide), LOW),
    ]


def net_call(kernel, ident, name, ins, outs, scratch=(), copies=64, late=()):
    fetched = [pltpu.VMEM(ins[i].shape, ins[i].dtype) for i in late]
    if late:
        fetched.append(pltpu.SemaphoreType.DMA((len(late),)))
    return pl.pallas_call(
        kernel,
        out_shape=[jax.ShapeDtypeStruct(s, t) for s, t in outs],
        in_specs=[
            pl.BlockSpec(memory_space=pl.ANY if i in late else pltpu.VMEM) for i in range(len(ins))
        ],
        out_specs=[pl.BlockSpec(memory_space=pltpu.VMEM)] * len(outs),
        scratch_shapes=[
            *scratch,
            *fetched,
            pltpu.SemaphoreType.DMA((copies,)),
            pltpu.SemaphoreType.DMA((copies,)),
        ],
        compiler_params=pltpu.CompilerParams(
            collective_id=ident, has_side_effects=True, vmem_limit_bytes=VMEM_LIMIT
        ),
        name=name,
    )(*ins)


def first_kernel(
    fused,
    x_ref, cot_ref, wq_ref, wo_ref, up_ref, down_ref, vec_ref,
    x_all, wq_all, up_mine, down_mine, vec_all, wo_all, *rest,
):
    cot_all = None if fused else rest[0]
    wo_got, send_sem, recv_sem = rest[-3:]
    net = Net(send_sem, recv_sem)
    d, c = net.d, net.c
    vec_all[d] = vec_ref[...]
    wq_all[d, c] = wq_ref[c]
    wo_got[c] = wo_ref[c]
    x_all[c] = x_ref[...]
    if not fused:
        cot_all[c] = cot_ref[...]
    net.greet()
    trade_q = Trade(net, wq_ref, lambda r: wq_all.at[d, r])
    vectors = PairGather(net, vec_all.at[d], lambda z: vec_all.at[pl.ds(z * 2, 2)])
    trade_o = Trade(net, wo_ref, lambda r: wo_got.at[r])
    share_x = Share(net, x_all)
    up_mine[c] = up_ref[c]
    down_mine[c] = down_ref[c]
    trade_q.received()
    gather_q = Gather(net, lambda z: wq_all.at[net.at(z)])
    trade_o.received()
    wo_mine = wo_all.at[d]
    room = wo_mine.shape[1] // net.ctx
    for r in range(net.ctx):
        wo_mine[:, r * room : (r + 1) * room] = wo_got[r, :, :room]
    gather_o = PairGather(net, wo_mine, lambda z: wo_all.at[pl.ds(z * 2, 2)])
    vectors.begin()
    share_x.forward()
    trade_up = Trade(net, up_ref, lambda r: up_mine.at[r])
    trade_down = Trade(net, down_ref, lambda r: down_mine.at[r])
    items = [trade_q, trade_o, vectors, share_x, gather_q, gather_o, trade_up, trade_down]
    if not fused:
        share_cot = Share(net, cot_all)
        share_cot.forward()
        items.append(share_cot)
    gather_q.step(0)
    vectors.step(0)
    gather_o.begin()
    for k in range(1, net.outer - 1):
        gather_q.step(k)
        gather_o.step(k - 1)
        vectors.step(k)
    gather_o.step(net.outer - 2)
    trade_up.received()
    trade_down.received()
    for item in items:
        item.finish()


def second_kernel(
    parts, x_ref, up_ref, down_ref, bias_ref, gain_ref, shift_ref,
    up_all, down_all, normed_all, residual_ref,
    near, held, far, send_sem, recv_sem,
):
    net = Net(send_sem, recv_sem)
    d, c = net.d, net.c
    up_all[d] = up_ref[...]
    down_all[d] = down_ref[...]
    net.greet()
    fold = Fold(net, parts, near, held, far)
    ff = down_all.shape[2]
    cut = pair_cut(ff)
    gather_up = Gather(net, lambda z: up_all.at[net.at(z)])
    pair_down = PairGather(
        net, down_all.at[d, :, pl.ds(0, cut)], lambda z: down_all.at[pl.ds(z * 2, 2), :, pl.ds(0, cut)]
    )
    fold.total(residual_ref)
    gather_up.step(0)
    pair_down.begin()
    gather_down = Gather(net, lambda z: down_all.at[net.at(z), :, pl.ds(cut, ff - cut)])
    residual = x_ref[...].astype(F32) + (residual_ref[...] + bias_ref[...])
    residual_ref[...] = residual
    scaled, _ = norm_stats(residual)
    normed_all[c] = (scaled * gain_ref[...] + shift_ref[...]).astype(LOW)
    share = Share(net, normed_all)
    for k in range(net.outer - 1):
        if k > 0:
            gather_up.step(k)
        if k == 0:
            share.forward()
        pair_down.step(k)
        gather_down.step(k)
    for item in (fold, share, gather_up, gather_down, pair_down):
        item.finish()


def third_kernel(
    parts, residual_ref, cot_ref, down_grad, up_grad, bias_ref, gain_ref,
    block_out, grad_residual, normed_grad, low_all, down_mine, up_mine,
    sums, near, held, far, near_down, passed_down, near_up, passed_up, acc_down, acc_up, send_sem, recv_sem,
):
    net = Net(send_sem, recv_sem)
    c = net.c
    net.greet()
    fold = Fold(net, parts, near, held, far)
    scatter_down = Scatter(net, lambda z, x: down_grad.at[z * 2 + x], near_down, passed_down, acc_down)
    scatter_down.step(0)
    fold.total(sums)
    rows = residual_ref.shape[0]
    residual = residual_ref[...]
    block_out[...] = (residual + (sums[pl.ds(0, rows)] + bias_ref[...])).astype(LOW)
    scaled, inverse = norm_stats(residual)
    upstream = sums[pl.ds(rows, rows)]
    normed_grad[...] = upstream
    total = cot_ref[...].astype(F32) + norm_backward(upstream, scaled, inverse, gain_ref[...])
    grad_residual[...] = total
    low_all[c] = total.astype(LOW)
    share = Share(net, low_all)
    for k in range(1, net.outer - 2):
        scatter_down.step(k)
    share.forward()
    scatter_up = Scatter(net, lambda z, x: up_grad.at[z * 2 + x], near_up, passed_up, acc_up)
    scatter_down.step(net.outer - 2)
    for k in range(net.outer - 1):
        scatter_up.step(k)
    scatter_down.total()
    down_mine[...] = acc_down[...].astype(LOW)
    scatter_up.total()
    up_mine[...] = acc_up[...].astype(LOW)
    for item in (fold, share, scatter_down, scatter_up):
        item.finish()


def last_kernel(
    parts, wq_grad, wo_grad, lines_ref, bias_lines, up_ref, down_ref, x_ref, residual_grad, gain_ref,
    grad_input, wq_back, wo_back, totals, up_back, down_back,
    sums, near, held, far, near_q, passed_q, near_o, passed_o, near_t, passed_t,
    acc_q, acc_o, acc_t, wq_mine, wo_mine, lines, table, table_all, send_sem, recv_sem,
):
    net = Net(send_sem, recv_sem)
    c = net.c
    net.greet()
    fold = Fold(net, parts, near, held, far)
    scatter_q = Scatter(net, lambda z, x: wq_grad.at[z * 2 + x], near_q, passed_q, acc_q)
    trade_up = Trade(net, up_ref, lambda g: up_back.at[g])
    trade_down = Trade(net, down_ref, lambda g: down_back.at[g])
    up_back[c] = up_ref[c]
    down_back[c] = down_ref[c]
    scatter_q.step(0)
    scaled, inverse = norm_stats(x_ref[...].astype(F32))
    fold.total(sums)
    upstream = sums[...]
    grad_input[...] = residual_grad[...] + norm_backward(upstream, scaled, inverse, gain_ref[...])
    lines[...] = lines_ref[...]
    lines[0:1] = jnp.sum(upstream * scaled, axis=0, keepdims=True)
    lines[1:2] = jnp.sum(upstream, axis=0, keepdims=True)
    lines[2 : 2 + bias_lines.shape[0]] = bias_lines[...]
    part = table.shape[2]
    for p in range(net.dp):
        table[p] = lines[:, p * part : (p + 1) * part]
    for k in range(1, net.outer - 2):
        scatter_q.step(k)
    scatter_o = Scatter(net, lambda z, x: wo_grad.at[z * 2 + x], near_o, passed_o, acc_o)
    scatter_t = Scatter(net, lambda z, x: table.at[z * 2 + x], near_t, passed_t, acc_t)
    scatter_q.step(net.outer - 2)
    for k in range(net.outer - 1):
        scatter_o.step(k)
        scatter_t.step(k)
    scatter_q.total()
    wq_mine[...] = acc_q[...].astype(LOW)
    trade_q = Trade(net, wq_mine, lambda g: wq_back.at[g])
    wq_back[c] = wq_mine[c]
    scatter_t.total()
    table_all[c] = acc_t[...]
    share_t = [
        net.send(table_all.at[c], table_all.at[c], ctx=lax.rem(c + step, net.ctx))
        for step in range(1, net.ctx)
    ]
    scatter_o.total()
    room = acc_o.shape[1] // net.ctx
    wo_mine[...] = jnp.zeros_like(wo_mine)
    for r in range(net.ctx):
        wo_mine[r, :, :room] = acc_o[:, r * room : (r + 1) * room].astype(LOW)
    trade_o = Trade(net, wo_mine, lambda g: wo_back.at[g])
    wo_back[c] = wo_mine[c]
    trades = (trade_up, trade_down, trade_q, trade_o)
    for item in trades:
        item.received()
    for copy in share_t:
        copy.wait_recv()
    total = table_all[0]
    for other in range(1, net.ctx):
        total = total + table_all[other]
    totals[...] = total
    for item in (fold, scatter_q, scatter_o, scatter_t, *trades):
        item.finish()
    for copy in share_t:
        copy.wait_send()


def pairs_of(ref, i):
    return jnp.concatenate([ref[2 * i], ref[2 * i + 1]], axis=1)


def causal(scores, first):
    rows = lax.broadcasted_iota(jnp.int32, scores.shape, 0) + first
    columns = lax.broadcasted_iota(jnp.int32, scores.shape, 1)
    return jnp.where(columns <= rows, scores, MASKED)


def attend_kernel(
    starts,
    x_all, cot_ref, wq_far, head_bias, head_pick_far, mixed_pick_far, wo_far, vec_ref, up_bias_ref,
    x_ref, up_ref, down_ref,
    cot_all, normed_one, heads, lse, mixed, mixed_slots, up_all, down_all, normed_all, residual_ref,
    hidden, slope, down_grad,
    projected, flat_mixed, wide_grad, parts, near, held, far,
    wq_ref, head_pick, mixed_pick, wo_ref, late_sem, send_sem, recv_sem,
):
    net = Net(send_sem, recv_sem)
    d, c = net.d, net.c
    up_all[d] = up_ref[...]
    down_all[d] = down_ref[...]
    cot_all[c] = cot_ref[...]
    net.greet()
    ff = down_all.shape[2]
    cut = pair_cut(ff)
    share_cot = Share(net, cot_all)
    late = (wq_far, head_pick_far, mixed_pick_far, wo_far)
    fetched = (wq_ref, head_pick, mixed_pick, wo_ref)
    loads = [
        pltpu.make_async_copy(one, two, late_sem.at[n])
        for n, (one, two) in enumerate(zip(late, fetched, strict=True))
    ]
    for load in loads:
        load.start()
    gather_up = Gather(net, lambda z: up_all.at[net.at(z)])
    pair_down = PairGather(
        net, down_all.at[d, :, pl.ds(0, cut)], lambda z: down_all.at[pl.ds(z * 2, 2), :, pl.ds(0, cut)]
    )
    ctx, rows, width = x_all.shape
    slot = wq_ref.shape[2]
    most = mixed.shape[0]
    factor = float(HEAD_DIM) ** (-0.5)

    def norm_block(b, carry):
        scaled, _ = norm_stats(x_all[b].astype(F32))
        normed_one[b] = (scaled * vec_ref[0:1] + vec_ref[1:2]).astype(LOW)
        return carry

    lax.fori_loop(0, ctx, norm_block, 0)
    for load in loads:
        load.wait()
    slot_bias = plain(head_bias[...], head_pick[...])[0:1]
    for i in range(net.dp // 2):
        weight = pairs_of(wq_ref, i)
        span = pl.ds(i * 2 * slot, 2 * slot)
        bias = slot_bias[:, i * 2 * slot : (i + 1) * 2 * slot]

        def project(b, carry):
            out = plain(normed_one[b], weight) + bias
            projected[b, :, span] = out.astype(LOW)
            return carry

        lax.fori_loop(0, ctx, project, 0)
    share_cot.forward()
    gather_up.step(0)
    pair_down.begin()

    def pick_block(b, carry):
        span = pl.ds(pl.multiple_of(b * rows, rows), rows)
        picked = outer_cols(projected[b], head_pick[...]).astype(LOW)
        for h in range(3 * most):
            heads[h, span] = picked[:, h * HEAD_DIM : (h + 1) * HEAD_DIM]
        return carry

    lax.fori_loop(0, ctx, pick_block, 0)

    def attend(i, carry):
        for b in range(ctx):
            here = slice(b * rows, (b + 1) * rows)
            past = slice(0, (b + 1) * rows)
            scores = outer_cols(heads[i, here], heads[most + i, past]) * factor
            scores = causal(scores, b * rows)
            peak = jnp.max(scores, axis=-1, keepdims=True)
            log_total = peak + jnp.log(jnp.sum(jnp.exp(scores - peak), axis=-1, keepdims=True))
            soft = jnp.exp(scores - log_total).astype(LOW)
            lse[i, here] = log_total
            mixed[i, here] = plain(soft, heads[2 * most + i, past]).astype(LOW)
        return carry

    lax.fori_loop(0, most, attend, 0)
    gather_up.step(1)
    pair_down.step(0)
    gather_down = Gather(net, lambda z: down_all.at[net.at(z), :, pl.ds(cut, ff - cut)])
    share_cot.finish()

    def out_block(b):
        span = pl.ds(pl.multiple_of(b * rows, rows), rows)
        for i in range(most):
            flat_mixed[:, i * HEAD_DIM : (i + 1) * HEAD_DIM] = mixed[i, span]
        mixed_slots[b] = plain(flat_mixed[...], mixed_pick[...]).astype(LOW)
        parts[b] = outer_cols(mixed_slots[b], wo_ref[...]).astype(LOW)

    fold = Fold(net, parts, near, held, far, out_block)
    for k in range(2, net.outer - 1):
        gather_up.step(k)
    fold.total(residual_ref)
    residual = x_ref[...].astype(F32) + (residual_ref[...] + vec_ref[starts[3] : starts[3] + 1])
    residual_ref[...] = residual
    scaled, _ = norm_stats(residual)
    gain, shift = vec_ref[starts[4] : starts[4] + 1], vec_ref[starts[5] : starts[5] + 1]
    normed_all[c] = (scaled * gain + shift).astype(LOW)
    share = Share(net, normed_all)
    gather_down.step(0)
    share.forward()
    pair_down.step(1)
    gather_down.step(1)
    share.finish()
    gather_up.finish()
    up_bias = up_bias_ref[pl.ds(c, 1)]
    up_flat = up_all[...].reshape(ff, width)

    def hidden_block(b, carry):
        pre = outer_cols(normed_all[b], up_flat) + up_bias
        bell = 0.5 * (1.0 + lax.erf(pre * INV_ROOT_TWO))
        hidden[pl.ds(pl.multiple_of(b * rows, rows), rows)] = (pre * bell).astype(LOW)
        slope[b] = bell + pre * jnp.exp(-0.5 * pre * pre) * INV_ROOT_TWO_PI
        return carry

    lax.fori_loop(0, ctx, hidden_block, 0)
    for k in range(2, net.outer - 1):
        gather_down.step(k)
        pair_down.step(k)
    part = down_grad.shape[1]
    cross(cot_all[...].reshape(ctx * rows, width), hidden[...], wide_grad)
    for p in range(net.dp):
        down_grad[p] = wide_grad[p * part : (p + 1) * part].astype(LOW)
    for item in (fold, gather_down, pair_down):
        item.finish()


def cross(left, right, out):
    for at in range(0, left.shape[1], 256):
        end = min(at + 256, left.shape[1])
        out[at:end] = inner_rows(left[:, at:end], right)


def return_kernel(
    starts,
    hidden, slope, down_grad,
    normed_ref, cot_all, up_flat, down_flat, residual_ref, cot_ref, vec_ref,
    *rest,
):
    late, rest = rest[:9], rest[9:]
    (
    block_out, grad_residual, lines, down_mine, up_mine, one_part, wq_grad, wo_grad, bias_sums,
    grad_hidden, up_total, wide_grad, up_grad, down_parts, parts,
    low_all, down_sums, down_near, down_held, down_far, sums, near, held, far, near_down, passed_down, near_up, passed_up, acc_down, acc_up,
    mixed_grad, grad_heads, flat_heads, grad_slots, key_total, value_total, *fetched, late_sem, send_sem, recv_sem,
    ) = rest
    wq_ref, head_pick, mixed_pick, wo_ref, normed_one, heads, lse, mixed, mixed_slots = fetched
    net = Net(send_sem, recv_sem)
    c = net.c
    net.greet()
    loads = [
        pltpu.make_async_copy(one, two, late_sem.at[n])
        for n, (one, two) in enumerate(zip(late, fetched, strict=True))
    ]
    scatter_down = Scatter(net, lambda z, x: down_grad.at[z * 2 + x], near_down, passed_down, acc_down)
    for load in loads:
        load.start()
    ctx, rows, _ = normed_ref.shape
    part = down_grad.shape[1]
    piece = up_grad.shape[1]
    tokens = ctx * rows

    def spanned(b):
        return pl.ds(pl.multiple_of(b * rows, rows), rows)

    up_total[...] = jnp.zeros_like(up_total)

    def back_block(b):
        down_parts[b] = outer_cols(hidden[spanned(b)], down_flat[...]).astype(LOW)
        grad = plain(cot_all[b], down_flat[...]) * slope[b]
        low = grad.astype(LOW)
        grad_hidden[spanned(b)] = low
        parts[b] = plain(low, up_flat[...]).astype(LOW)
        up_total[...] += jnp.sum(grad, axis=0, keepdims=True)

    fold = Fold(net, parts, near, held, far, back_block)
    up_sum = up_total[...]
    scatter_down.step(0)
    normed_two = normed_ref[...].reshape(tokens, normed_ref.shape[2])
    grad_low = grad_hidden[...]
    cross(grad_low, normed_two, wide_grad)
    for p in range(net.dp):
        up_grad[p] = wide_grad[p * piece : (p + 1) * piece].astype(LOW)
    scatter_up = Scatter(net, lambda z, x: up_grad.at[z * 2 + x], near_up, passed_up, acc_up)
    fold.total(sums)
    residual = residual_ref[...]
    gain = vec_ref[starts[4] : starts[4] + 1]
    scaled, inverse = norm_stats(residual)
    upstream = sums[...]
    own_cot = cot_ref[...].astype(F32)
    total = own_cot + norm_backward(upstream, scaled, inverse, gain)
    grad_residual[...] = total
    low_all[c] = total.astype(LOW)
    share = Share(net, low_all)
    down_fold = Fold(net, down_parts, down_near, down_held, down_far)

    def line(value):
        return jnp.sum(value, axis=0, keepdims=True)

    lines[...] = jnp.zeros_like(lines)
    lines[starts[3] : starts[3] + 1] = line(total)
    lines[starts[4] : starts[4] + 1] = line(upstream * scaled)
    lines[starts[5] : starts[5] + 1] = line(upstream)
    for p in range(net.dp):
        span = slice(p * part, (p + 1) * part)
        lines[pl.ds(starts[6] + c, 1), span] = up_sum[:, p * piece : p * piece + part]
    lines[starts[7] : starts[7] + 1] = line(own_cot)
    for k in range(1, net.outer - 2):
        scatter_down.step(k)
    share.forward()
    share.finish()
    scatter_down.step(net.outer - 2)
    for load in loads:
        load.wait()
    most = mixed.shape[0]
    slot = wq_ref.shape[2]
    factor = float(HEAD_DIM) ** (-0.5)

    def mixed_block(b, carry):
        slots = plain(low_all[b], wo_ref[...]).astype(LOW)
        picked = outer_cols(slots, mixed_pick[...]).astype(LOW)
        for i in range(most):
            mixed_grad[i, spanned(b)] = picked[:, i * HEAD_DIM : (i + 1) * HEAD_DIM]
        return carry

    lax.fori_loop(0, ctx, mixed_block, 0)

    def attend_back(i, carry):
        query_sum = jnp.zeros((1, HEAD_DIM), F32)
        for b in range(ctx - 1, -1, -1):
            here = slice(b * rows, (b + 1) * rows)
            past = slice(0, (b + 1) * rows)
            query, key, value = heads[i, here], heads[most + i, past], heads[2 * most + i, past]
            scores = causal(outer_cols(query, key) * factor, b * rows)
            probs = jnp.exp(scores - lse[i, here])
            upper = mixed_grad[i, here]
            delta = jnp.sum(upper.astype(F32) * mixed[i, here].astype(F32), axis=-1, keepdims=True)
            grad_scores = (probs * (outer_cols(upper, value) - delta) * factor).astype(LOW)
            grad_query = plain(grad_scores, key)
            query_sum = query_sum + jnp.sum(grad_query, axis=0, keepdims=True)
            grad_heads[i, here] = grad_query.astype(LOW)
            key_part = inner_rows(grad_scores, query)
            value_part = inner_rows(probs.astype(LOW), upper)
            if b == ctx - 1:
                key_total[...] = key_part
                value_total[...] = value_part
            else:
                key_total[past] += key_part
                value_total[past] += value_part
        grad_heads[most + i] = key_total[...].astype(LOW)
        grad_heads[2 * most + i] = value_total[...].astype(LOW)
        bias_sums[i] = query_sum
        bias_sums[most + i] = jnp.sum(value_total[...], axis=0, keepdims=True)
        return carry

    lax.fori_loop(0, 2, attend_back, 0)
    down_fold.total(down_sums)
    down_bias = vec_ref[starts[7] : starts[7] + 1]
    block_out[...] = (residual_ref[...] + (down_sums[...] + down_bias)).astype(LOW)
    scatter_up.step(0)
    lax.fori_loop(2, most, attend_back, 0)
    for k in range(1, net.outer - 2):
        scatter_up.step(k)

    def slot_block(b, carry):
        span = spanned(b)
        for h in range(3 * most):
            flat_heads[:, h * HEAD_DIM : (h + 1) * HEAD_DIM] = grad_heads[h, span]
        grad_slots[span] = plain(flat_heads[...], head_pick[...]).astype(LOW)
        total = outer_cols(grad_slots[span, : 2 * slot], pairs_of(wq_ref, 0))
        for i in range(1, net.dp // 2):
            part = grad_slots[span, i * 2 * slot : (i + 1) * 2 * slot]
            total = total + outer_cols(part, pairs_of(wq_ref, i))
        one_part[b] = total.astype(LOW)
        return carry

    lax.fori_loop(0, ctx, slot_block, 0)
    scatter_up.step(net.outer - 2)
    normed = normed_one[...]
    for i in range(net.dp // 2):
        weight_grad = inner_rows(normed, grad_slots[:, i * 2 * slot : (i + 1) * 2 * slot])
        wq_grad[2 * i] = weight_grad[:, :slot].astype(LOW)
        wq_grad[2 * i + 1] = weight_grad[:, slot:].astype(LOW)
    weight_grad = inner_rows(low_all[0], mixed_slots[0])
    for b in range(1, ctx):
        weight_grad = weight_grad + inner_rows(low_all[b], mixed_slots[b])
    wo_grad[...] = weight_grad.astype(LOW)
    scatter_down.total()
    down_mine[...] = acc_down[...].astype(LOW)
    scatter_up.total()
    up_mine[...] = acc_up[...].astype(LOW)
    for item in (fold, down_fold, scatter_down, scatter_up):
        item.finish()


def pair_cut(lanes):
    return rounded_up(lanes // 3, 128)


def attention(x_flat, gain, shift, wq, bias_slots, head_pick, mixed_pick, wo, most):
    tokens = x_flat.shape[0]
    factor = float(HEAD_DIM) ** (-0.5)
    scaled, _ = norm_stats(x_flat.astype(F32))
    normed = (scaled * gain + shift).astype(LOW)
    projected = jnp.einsum("tk,dks->tds", normed, wq, preferred_element_type=F32)
    projected = (projected.reshape(tokens, -1) + bias_slots).astype(LOW)
    heads = outer_cols(projected, head_pick).astype(LOW)
    heads = heads.reshape(tokens, 3, most, HEAD_DIM).transpose(1, 2, 0, 3)
    queries, keys, values = heads[0], heads[1], heads[2]
    index = jnp.arange(tokens, dtype=jnp.int32)
    scores = jnp.einsum("hqd,hkd->hqk", queries, keys, preferred_element_type=F32) * factor
    scores = jnp.where(index[None, :] <= index[:, None], scores, MASKED)
    peak = jnp.max(scores, axis=-1, keepdims=True)
    log_total = peak + jnp.log(jnp.sum(jnp.exp(scores - peak), axis=-1, keepdims=True))
    probs = jnp.exp(scores - log_total)
    soft = probs.astype(LOW)
    mixed = jnp.einsum("hqk,hkd->hqd", soft, values, preferred_element_type=F32).astype(LOW)
    mixed_flat = mixed.transpose(1, 0, 2).reshape(tokens, most * HEAD_DIM)
    mixed_slots = plain(mixed_flat, mixed_pick).astype(LOW)
    out_part = outer_cols(mixed_slots, wo).astype(LOW)
    return normed, queries, keys, values, probs, soft, mixed, mixed_slots, out_part


def attention_back(
    low, normed, queries, keys, values, probs, soft, mixed, mixed_slots, wq, wo, head_pick, mixed_pick
):
    most, tokens = mixed.shape[:2]
    dp, _, slot = wq.shape
    factor = float(HEAD_DIM) ** (-0.5)
    grad_mixed = outer_cols(plain(low, wo).astype(LOW), mixed_pick).astype(LOW)
    grad_mixed = grad_mixed.reshape(tokens, most, HEAD_DIM).transpose(1, 0, 2)
    grad_probs = jnp.einsum("hqd,hkd->hqk", grad_mixed, values, preferred_element_type=F32)
    delta = jnp.sum(grad_mixed.astype(F32) * mixed.astype(F32), axis=-1, keepdims=True)
    grad_scores = (probs * (grad_probs - delta) * factor).astype(LOW)
    grad_q = jnp.einsum("hqk,hkd->hqd", grad_scores, keys, preferred_element_type=F32)
    grad_k = jnp.einsum("hqk,hqd->hkd", grad_scores, queries, preferred_element_type=F32)
    grad_v = jnp.einsum("hqk,hqd->hkd", soft, grad_mixed, preferred_element_type=F32)
    bias_sums = jnp.sum(jnp.stack([grad_q, grad_v]), axis=2)
    grad_heads = jnp.stack([grad_q, grad_k, grad_v]).astype(LOW)
    grad_heads = grad_heads.transpose(2, 0, 1, 3).reshape(tokens, 3 * most * HEAD_DIM)
    grad_slots = plain(grad_heads, head_pick).astype(LOW).reshape(tokens, dp, slot)
    one_part = jnp.einsum("tds,dks->tk", grad_slots, wq, preferred_element_type=F32).astype(LOW)
    wq_grad = jnp.einsum("tk,tds->dks", normed, grad_slots, preferred_element_type=F32).astype(LOW)
    wo_grad = inner_rows(low, mixed_slots).astype(LOW)
    return one_part, wq_grad, wo_grad, bias_sums


def on_device(
    block_input,
    norm_one_gain,
    norm_one_bias,
    w_qkv,
    bias_qv,
    w_out,
    bias_out,
    norm_two_gain,
    norm_two_bias,
    w_up,
    bias_up,
    w_down,
    bias_down,
    cotangent,
):
    seq_count, block_len, width = block_input.shape
    rows = seq_count * block_len
    ctx = lax.axis_size("ctx")
    dp = lax.axis_size("dp")
    d, c = lax.axis_index("dp"), lax.axis_index("ctx")
    fold = dp // ctx
    outer = dp // 2
    tokens = rows * ctx
    grad_scale = float(tokens * dp) ** (-0.5)
    factor = float(HEAD_DIM) ** (-0.5)
    high, wide = w_qkv.shape
    part = w_out.shape[1]
    units = w_up.shape[1]
    share_units = units // ctx

    tables = slot_tables(width, dp, ctx)
    most, slot, row_slot = tables["most"], tables["slot"], tables["row_slot"]
    mixed_wide = ctx * tables["row_pack"]

    column_pick = picker(tables["column_pick"], d, wide)
    row_pick = picker(tables["row_pick"], c, high)

    wq = plain(w_qkv, column_pick).astype(LOW).reshape(high, ctx, slot).transpose(1, 0, 2)
    wo = inner_rows(w_out, row_pick).astype(LOW).reshape(part, ctx, row_slot).transpose(1, 0, 2)
    up = w_up.T.reshape(ctx, share_units, high)
    down = (
        w_down.reshape(fold, ctx, share_units, part)
        .transpose(1, 3, 0, 2)
        .reshape(ctx, part, fold * share_units)
    )
    pieces = (
        norm_one_gain,
        norm_one_bias,
        bias_qv,
        bias_out,
        norm_two_gain,
        norm_two_bias,
        bias_up,
        bias_down,
    )
    lines = [v.shape[0] // part for v in pieces]
    line_count = sum(lines)
    line_room = rounded_up(line_count, 16)
    *pieces, wq, wo, up, down = lax.optimization_barrier((*pieces, wq, wo, up, down))
    vec = jnp.concatenate([*pieces, jnp.zeros(((line_room - line_count) * part,), LOW)])
    vec = vec.reshape(line_room, part)

    x_own = block_input.reshape(rows, width)
    cot_own = cotangent.reshape(rows, width)

    fused = dp * slot <= 2048
    x_all, wq_all, up_mine, down_mine, vec_all, wo_all, *more = net_call(
        functools.partial(first_kernel, fused),
        0,
        "gather_first",
        (x_own, cot_own, wq, wo, up, down, vec),
        [
            ((ctx, rows, width), LOW),
            ((dp, ctx, high, slot), LOW),
            (up.shape, LOW),
            (down.shape, LOW),
            ((dp, line_room, part), LOW),
            ((dp, part, mixed_wide), LOW),
            *([] if fused else [((ctx, rows, width), LOW)]),
        ],
        scratch=[pltpu.VMEM((ctx, part, row_slot), LOW)],
        copies=12 * outer + 64,
    )

    room = rounded_up(share_units, 16)
    extra = room - share_units
    ff = dp * room
    ups = jnp.pad(up_mine.transpose(1, 0, 2).reshape(share_units, width), ((0, extra), (0, 0)))
    downs = down_mine.transpose(1, 0, 2).reshape(part, dp, share_units)
    downs = jnp.pad(downs, ((0, 0), (0, 0), (0, extra))).reshape(part, ff)

    across = vec_all.transpose(1, 0, 2).reshape(line_room, width).astype(F32)
    starts = np.cumsum([0] + lines)
    starts = [int(v) for v in starts]
    up_bias = jnp.pad(vec_all[:, starts[6] : starts[7]], ((0, 0), (0, 0), (0, extra)))
    up_bias = up_bias.transpose(1, 0, 2).reshape(ctx, ff).astype(F32)
    bias_q_v = vec_all[:, starts[2] : starts[3]].reshape(2, HEADS, HEAD_DIM)

    head_rows = lax.dynamic_index_in_dim(jnp.asarray(tables["head_rows"]), c, 0, keepdims=False)
    head_hot = head_rows[:, None] == jnp.arange(HEADS, dtype=jnp.int32)[None, :]
    bias_heads = jnp.einsum("ih,thf->tif", head_hot.astype(LOW), bias_q_v, preferred_element_type=F32)
    bias_heads = jnp.concatenate(
        [bias_heads[:1], jnp.zeros_like(bias_heads[:1]), bias_heads[1:]]
    ).reshape(1, -1)

    wq_flat = wq_all.reshape(dp, width, slot)
    head_pick = row_picker(tables["head_pick"], c, dp * slot)
    mixed_pick = row_picker(tables["mixed_pick"], c, mixed_wide)
    wo_flat = wo_all.reshape(width, mixed_wide)
    if fused:
        (
            cot_all, normed_one, heads, lse, mixed, mixed_slots, up_all, down_all, normed_two,
            residual, hidden, slope, down_grad,
        ) = net_call(
            functools.partial(attend_kernel, starts),
            1,
            "attend_second",
            (
                x_all, cot_own, wq_flat, jnp.tile(bias_heads.astype(LOW), (16, 1)), head_pick,
                mixed_pick, wo_flat, across, up_bias, x_own, ups, downs,
            ),
            [
                ((ctx, rows, width), LOW),
                ((ctx, rows, width), LOW),
                ((3 * most, tokens, HEAD_DIM), LOW),
                ((most, tokens, 1), F32),
                ((most, tokens, HEAD_DIM), LOW),
                ((ctx, rows, mixed_wide), LOW),
                ((dp, room, width), LOW),
                ((dp, part, ff), LOW),
                ((ctx, rows, width), LOW),
                ((rows, width), F32),
                ((tokens, ff), LOW),
                ((ctx, rows, ff), F32),
                ((dp, part, ff), LOW),
            ],
            scratch=[
                pltpu.VMEM((ctx, rows, dp * slot), LOW),
                pltpu.VMEM((rows, most * HEAD_DIM), LOW),
                pltpu.VMEM((width, ff), F32),
                pltpu.VMEM((ctx, rows, width), LOW),
                *fold_scratch(rows, width),
            ],
            late=(2, 4, 5, 6),
            copies=18 * outer + 64,
        )
    else:
        cot_all = more[0]
        normed_one, queries, keys, values, probs, soft_weights, mixed, mixed_slots, out_part = attention(
            x_all.reshape(tokens, width), across[0:1], across[1:2], wq_flat,
            plain(bias_heads.astype(LOW), head_pick), head_pick, mixed_pick, wo_flat, most,
        )
        up_all, down_all, normed_two, residual = net_call(
            second_kernel,
            1,
            "gather_second",
            (
                out_part.reshape(ctx, rows, width), x_own, ups, downs,
                *[across[starts[i] : starts[i] + 1] for i in (3, 4, 5)],
            ),
            [
                ((dp, room, width), LOW),
                ((dp, part, ff), LOW),
                ((ctx, rows, width), LOW),
                ((rows, width), F32),
            ],
            scratch=fold_scratch(rows, width),
            copies=12 * outer + 64,
        )
    up_flat = up_all.reshape(ff, width)
    down_flat = down_all.reshape(width, ff)
    third_scratch = [
        pltpu.VMEM((2 * rows, width), F32),
        *fold_scratch(2 * rows, width),
        pltpu.VMEM((outer, part, ff), LOW),
        pltpu.VMEM((outer + 1, part, ff), LOW),
        pltpu.VMEM((outer, room, width), LOW),
        pltpu.VMEM((outer + 1, room, width), LOW),
        pltpu.VMEM((part, ff), F32),
        pltpu.VMEM((room, width), F32),
    ]
    third_sums = [((part, ff), LOW), ((room, width), LOW)]
    if fused:
        (
            block_output, grad_residual, small, down_sum, up_sum,
            one_part, wq_grad, wo_grad, bias_sums,
        ) = net_call(
            functools.partial(return_kernel, starts),
            2,
            "return_third",
            (
                hidden, slope, down_grad,
                normed_two, cot_all, up_flat, down_flat, residual, cot_own, across,
                wq_flat, head_pick, mixed_pick, wo_flat,
                normed_one.reshape(tokens, width), heads, lse, mixed, mixed_slots,
            ),
            [
                ((rows, width), LOW),
                ((rows, width), F32),
                ((line_room, width), F32),
                *third_sums,
                ((ctx, rows, width), LOW),
                ((dp, width, slot), LOW),
                ((width, mixed_wide), LOW),
                ((2 * most, 1, HEAD_DIM), F32),
            ],
            scratch=[
                pltpu.VMEM((tokens, ff), LOW),
                pltpu.VMEM((1, ff), F32),
                pltpu.VMEM((ff, width), F32),
                pltpu.VMEM((dp, room, width), LOW),
                *[pltpu.VMEM((ctx, rows, width), LOW)] * 3,
                pltpu.VMEM((rows, width), F32),
                *fold_scratch(rows, width),
                pltpu.VMEM((rows, width), F32),
                *fold_scratch(rows, width),
                *third_scratch[4:],
                pltpu.VMEM((most, tokens, HEAD_DIM), LOW),
                pltpu.VMEM((3 * most, tokens, HEAD_DIM), LOW),
                pltpu.VMEM((rows, 3 * most * HEAD_DIM), LOW),
                pltpu.VMEM((tokens, dp * slot), LOW),
                pltpu.VMEM((tokens, HEAD_DIM), F32),
                pltpu.VMEM((tokens, HEAD_DIM), F32),
            ],
            copies=6 * outer + 64,
            late=range(10, 19),
        )
        bias_sums = bias_sums.reshape(2, most, HEAD_DIM)
    else:
        normed_two = normed_two.reshape(tokens, width)
        cot_flat = cot_all.reshape(tokens, width)
        hidden_pre = outer_cols(normed_two, up_flat) + lax.dynamic_slice_in_dim(up_bias, c, 1, axis=0)
        hidden = gelu_value(hidden_pre).astype(LOW)
        down_part = outer_cols(hidden, down_flat).astype(LOW).reshape(ctx, rows, width)
        grad_hidden = plain(cot_flat, down_flat) * gelu_slope(hidden_pre)
        grad_hidden_low = grad_hidden.astype(LOW)
        normed_part = plain(grad_hidden_low, up_flat).astype(LOW).reshape(ctx, rows, width)
        down_grad = inner_rows(cot_flat, hidden).astype(LOW).reshape(dp, part, ff)
        up_grad = inner_rows(grad_hidden_low, normed_two).astype(LOW).reshape(dp, room, width)
        block_output, grad_residual, grad_normed_two, low_all, down_sum, up_sum = net_call(
            third_kernel,
            2,
            "scatter_third",
            (
                jnp.concatenate([down_part, normed_part], axis=1),
                residual,
                cot_own,
                down_grad,
                up_grad,
                across[starts[7] : starts[7] + 1],
                across[starts[4] : starts[4] + 1],
            ),
            [
                ((rows, width), LOW),
                ((rows, width), F32),
                ((rows, width), F32),
                ((ctx, rows, width), LOW),
                *third_sums,
            ],
            scratch=third_scratch,
            copies=6 * outer + 64,
        )
        one_part, wq_grad, wo_grad, bias_sums = attention_back(
            low_all.reshape(tokens, width), normed_one, queries, keys, values, probs, soft_weights,
            mixed, mixed_slots, wq_flat, wo_flat, head_pick, mixed_pick,
        )
        one_part = one_part.reshape(ctx, rows, width)
        scaled_two, _ = norm_stats(residual)
        up_lines = jnp.where(
            jnp.arange(ctx, dtype=jnp.int32)[:, None] == c,
            jnp.sum(grad_hidden, axis=0).reshape(dp, room)[:, :share_units].reshape(1, width),
            0.0,
        )
        small = jnp.concatenate(
            [
                jnp.zeros((starts[3], width), F32),
                jnp.sum(grad_residual, axis=0)[None],
                jnp.sum(grad_normed_two * scaled_two, axis=0)[None],
                jnp.sum(grad_normed_two, axis=0)[None],
                up_lines,
                jnp.sum(cot_own.astype(F32), axis=0)[None],
                jnp.zeros((line_room - line_count, width), F32),
            ]
        )
    wq_grad = wq_grad.reshape(dp, ctx, high, slot)
    wo_grad = wo_grad.reshape(dp, part, mixed_wide)

    bias_grad = jnp.einsum(
        "ih,tif->thf", head_hot.astype(F32), bias_sums, precision=lax.Precision.HIGHEST
    )
    bias_lines = bias_grad.reshape(dp, -1, part).transpose(1, 0, 2).reshape(-1, width)
    back_up = up_sum[:share_units].reshape(share_units, ctx, high).transpose(1, 0, 2)
    back_down = down_sum.T.reshape(dp, room, part)[:, :share_units]
    back_down = back_down.reshape(ctx, fold * share_units, part)

    grad_input, wq_back, wo_back, totals, up_back, down_back = net_call(
        last_kernel,
        3,
        "scatter_last",
        (
            one_part, wq_grad, wo_grad, small, bias_lines, back_up, back_down, x_own, grad_residual,
            across[0:1],
        ),
        [
            ((rows, width), F32),
            ((ctx, high, slot), LOW),
            ((ctx, part, row_slot), LOW),
            ((line_room, part), F32),
            (back_up.shape, LOW),
            (back_down.shape, LOW),
        ],
        scratch=[
            pltpu.VMEM((rows, width), F32),
            *fold_scratch(rows, width),
            *[pltpu.VMEM((outer + i, ctx, high, slot), LOW) for i in (0, 1)],
            *[pltpu.VMEM((outer + i, part, mixed_wide), LOW) for i in (0, 1)],
            *[pltpu.VMEM((outer + i, line_room, part), F32) for i in (0, 1)],
            pltpu.VMEM((ctx, high, slot), F32),
            pltpu.VMEM((part, mixed_wide), F32),
            pltpu.VMEM((line_room, part), F32),
            pltpu.VMEM((ctx, high, slot), LOW),
            pltpu.VMEM((ctx, part, row_slot), LOW),
            pltpu.VMEM((line_room, width), F32),
            pltpu.VMEM((dp, line_room, part), F32),
            pltpu.VMEM((ctx, line_room, part), F32),
        ],
        copies=9 * outer + 64,
    )
    wq_rows = wq_back.transpose(1, 0, 2).reshape(high, ctx * slot)
    grad_qkv = outer_cols(wq_rows, column_pick) * grad_scale
    wo_rows = wo_back.transpose(1, 0, 2).reshape(part, ctx * row_slot)
    grad_out = outer_cols(row_pick, wo_rows) * grad_scale
    grad_up = up_back.reshape(units, high).T.astype(F32) * grad_scale
    grad_down = (
        down_back.reshape(ctx, fold, share_units, part)
        .transpose(1, 0, 2, 3)
        .reshape(w_down.shape)
        .astype(F32)
        * grad_scale
    )
    totals = totals * grad_scale
    owned = [totals[starts[i] : starts[i + 1]].reshape(-1) for i in range(len(lines))]
    return (
        block_input_like(block_output, seq_count, block_len),
        block_input_like(grad_input, seq_count, block_len),
        owned[0],
        owned[1],
        grad_qkv,
        owned[2],
        grad_out,
        owned[3],
        owned[4],
        owned[5],
        grad_up,
        owned[6],
        grad_down,
        owned[7],
    )


def block_input_like(flat, seq_count, block_len):
    return flat.reshape(seq_count, block_len, flat.shape[-1])


def solution(mesh):
    in_specs = (
        P("dp", "ctx", None),
        P("dp"),
        P("dp"),
        P("ctx", "dp"),
        P("dp"),
        P("ctx", "dp"),
        P("dp"),
        P("dp"),
        P("dp"),
        P("ctx", "dp"),
        P("dp"),
        P("ctx", "dp"),
        P("dp"),
        P("dp", "ctx", None),
    )
    out_specs = (
        P("dp", "ctx", None),
        P("dp", "ctx", None),
        P("dp"),
        P("dp"),
        P("ctx", "dp"),
        P("dp"),
        P("ctx", "dp"),
        P("dp"),
        P("dp"),
        P("dp"),
        P("ctx", "dp"),
        P("dp"),
        P("ctx", "dp"),
        P("dp"),
    )
    return jax.shard_map(
        on_device, mesh=mesh, in_specs=in_specs, out_specs=out_specs, check_vma=False
    )
```
